512 devices in a mesh: seq: 64 (over z, y), ch: 8 (over x, core).
Axes of the slice: x: 4, y: 4, z: 16, core: 2. Of those that a mesh axis runs over, the one named last changes fastest.
Arguments:
- q_proj: bfloat16 [8192, 4096], P('seq', 'ch'), may hold values from -16 to 16
- k_proj: bfloat16 [8192, 4096], P('seq', 'ch'), may hold values from -6 to 6
- v_proj: bfloat16 [8192, 4096], P('seq', 'ch'), may hold values from -6 to 6
- feat_filter: float32 [3, 3, 4096], P(None, None, 'ch'), may hold values from -3.5 to 3.5
- long_filter: float32 [8192, 4096], P('seq', 'ch'), may hold values from -0.0625 to 0.0625
- skip_bias: float32 [4096], P('ch'), may hold values from -4 to 4
- norm_gain: float32 [4096], P('ch'), may hold values from 0.1 to 1.9
Outputs:
- mixed_out: bfloat16 [8192, 4096], P('seq', 'ch')
- normed: bfloat16 [8192, 4096], P('seq', 'ch')
The draws below stay inside these ranges and needn't reach their ends.
All inputs are finite; a program needn't handle non-finite values.
Results may differ from the reference program's by a relative error of at most 0.015.
Values may be sent and summed in bfloat16 or wider, within the bound.
No kernel may reach another device: no remote copies, remote signals or barrier semaphores. Data moves between devices by JAX's collectives and lax.ppermute only.
A program may use at most 64 MiB of HBM per device.

```python
import math
import jax
import jax.numpy as jnp
from jax import lax

D = 4096
FEAT = 3
SEQ = 8192


def draw_q_proj(key, part):
    ramp = 1.0 + 2.0 * jnp.arange(D, dtype=jnp.float32) / (D - 1)
    base = jax.random.truncated_normal(key, -4.0, 4.0, (SEQ, D), jnp.float32)
    return (base * ramp[None, :]).astype(jnp.bfloat16)


def steps_of(stream_key, shape, cuts, low, top_value):
    loudness, own = 1.0, jax.random.fold_in(stream_key, 6)
    for axis_at, parts in cuts:
        draws = jnp.exp(jax.random.uniform(jax.random.fold_in(own, axis_at), (parts,), jnp.float32, low / len(cuts), top_value / len(cuts)))
        loudness = loudness * jnp.repeat(draws, shape[axis_at] // parts).reshape([-1 if axis == axis_at else 1 for axis in range(len(shape))])
    return loudness


def normal_values(stream_key, dims, scale, limit, cuts=(), held_as=jnp.bfloat16):
    level = steps_of(stream_key, dims, cuts, -0.22, 0.18) if cuts else 1.0
    values = jax.random.normal(stream_key, dims, jnp.float32) * scale * level
    return jnp.minimum(jnp.maximum(values, -limit), limit).astype(held_as)


def setup_inputs(seed: int = 0) -> dict:
    key_list = jax.random.split(jax.random.key(seed), 8)
    q_proj = draw_q_proj(jax.random.fold_in(key_list[7], 71), 0)
    k_proj = normal_values(key_list[1], (SEQ, D), 1.0, 6.0, ((0, 64), (1, 8)))
    v_proj = normal_values(key_list[2], (SEQ, D), 1.0, 6.0, ((0, 64), (1, 8)))
    feat_filter = normal_values(key_list[3], (3, FEAT, D), FEAT ** -0.5, 3.5, ((2, 8),), jnp.float32)
    long_filter = normal_values(key_list[4], (SEQ, D), SEQ ** -0.5, 0.0625, ((0, 64), (1, 8)), jnp.float32)
    skip_bias = normal_values(key_list[5], (D,), 1.0, 4.0, ((0, 8),), jnp.float32)
    norm_gain = jnp.clip(1.0 + 0.18 * jax.random.normal(key_list[6], (D,), jnp.float32), 0.1, 1.9)
    return {"q_proj": q_proj, "k_proj": k_proj, "v_proj": v_proj, "feat_filter": feat_filter, "long_filter": long_filter, "skip_bias": skip_bias, "norm_gain": norm_gain}


def block_layer(query, keyed, valued, short_taps, filt, bias):
    stacked = jnp.stack([query, keyed, valued]).astype(jnp.float32)
    length = stacked.shape[1]
    taps = short_taps.shape[1]
    padded = jnp.pad(stacked, ((0, 0), (taps - 1, 0), (0, 0)))
    featured = jnp.zeros(stacked.shape, jnp.float32)
    for offset in range(taps):
        featured = featured + short_taps[:, offset, None, :] * padded[:, taps - 1 - offset:taps - 1 - offset + length, :]
    gated = featured[1] * featured[2]
    total = 2 * length
    spectrum = jnp.fft.rfft(gated, n=total, axis=0) * jnp.fft.rfft(filt, n=total, axis=0)
    long_conv = jnp.fft.irfft(spectrum, n=total, axis=0)[:length]
    return featured[0] * (long_conv + bias * gated)

def reference(q_proj, k_proj, v_proj, feat_filter, long_filter, skip_bias, norm_gain):
    width = math.gcd(D, 512)
    count = D // width

    def split(array):
        return array.reshape(SEQ, count, width).transpose(1, 0, 2)
    filters = feat_filter.reshape(3, FEAT, count, width).transpose(2, 0, 1, 3)
    biases = skip_bias.reshape(count, width)

    def one_block(pieces):
        return block_layer(pieces[0], pieces[1], pieces[2], pieces[3], pieces[4], pieces[5])
    mixed = lax.map(one_block, (split(q_proj), split(k_proj), split(v_proj), filters, split(long_filter), biases))
    mixed = mixed.transpose(1, 0, 2).reshape(SEQ, D)
    squares = lax.optimization_barrier(jnp.sum(mixed * mixed, axis=1, keepdims=True))
    scale = lax.rsqrt(squares / D + 1e-05)
    return (mixed.astype(jnp.bfloat16), (mixed * scale * norm_gain).astype(jnp.bfloat16))
```

```python
import jax
import jax.numpy as jnp
from jax import lax
from jax.experimental import pallas as pl
from jax.experimental.pallas import tpu as pltpu
from jax.sharding import PartitionSpec as P

EPS = 1e-05
F32 = jnp.float32
BF16 = jnp.bfloat16
VMEM = pl.BlockSpec(memory_space=pltpu.VMEM)


def shift_down(block, count):
    return jnp.concatenate([jnp.zeros((count, block.shape[1]), block.dtype), block[:-count]], axis=0)


def featured(stream_ref, halo, taps_ref, stream, padded):
    rows = stream_ref.shape[0]
    block = stream_ref[...].astype(F32)
    padded[8:, :] = block
    padded[6:8, :] = halo.astype(F32)
    out = taps_ref[stream, 0:1, :] * block
    out = out + taps_ref[stream, 1:2, :] * padded[7 : 7 + rows, :]
    return out + taps_ref[stream, 2:3, :] * padded[6 : 6 + rows, :]


def before_kernel(k_ref, v_ref, halo_ref, taps_ref, filter_ref, sent_ref, gated_ref, padded):
    rows, channels = k_ref.shape
    groups = sent_ref.shape[0]
    key = featured(k_ref, halo_ref[2:4, :], taps_ref, 1, padded)
    value = featured(v_ref, halo_ref[4:6, :], taps_ref, 2, padded)
    gated = key * value
    gated_ref[...] = gated
    down = lax.broadcasted_iota(jnp.int32, (rows, rows), 0)
    across = lax.broadcasted_iota(jnp.int32, (rows, rows), 1)
    backwards = (down + across == rows - 1).astype(BF16)
    taps = jnp.dot(backwards, filter_ref[...].astype(BF16), preferred_element_type=F32)
    signal = gated.T.reshape(groups, channels // groups, rows)
    taps = taps.T.reshape(groups, channels // groups, rows)
    sent_ref[...] = jnp.concatenate([signal, taps], axis=1).astype(BF16)


def conv_kernel(got_ref, out_ref, signal, taps, result):
    blocks, both, size = got_ref.shape
    each = both // 2
    half = size // 2
    got = got_ref[...].astype(F32)
    signal[...] = got[:, :each, :].reshape(blocks * each, size)
    taps[...] = got[:, each:, :].reshape(blocks * each, size)
    row = lax.broadcasted_iota(jnp.int32, (half, size), 0)
    lane = lax.broadcasted_iota(jnp.int32, (half, size), 1)
    own = lane < row + half + 1
    low = lane < half
    column = lane % half

    def channel(c, carry):
        now = signal[pl.ds(c, blocks, stride=each), :]
        once = shift_down(now, 1)
        twice = shift_down(now, 2)
        now_r, once_r, twice_r = (pltpu.roll(a, half, 1) for a in (now, once, twice))
        first = jnp.concatenate([jnp.where(low, twice_r, once_r), jnp.where(low, once_r, now_r)], axis=1)
        second = jnp.concatenate([once, now], axis=1)
        windows = jnp.concatenate([first, second], axis=0).astype(BF16)
        total = jnp.zeros((half, size), F32)
        before = jnp.zeros((half, size), F32)
        below = None
        for d in range(blocks):
            spread = jnp.broadcast_to(taps[pl.ds(each * d + c, 1), :], (half, size))
            turned = pltpu.roll(spread, half + 1, 1, stride=1, stride_axis=0)
            toeplitz = jnp.where(own, turned, before).astype(BF16)
            before = turned
            if d % 2 == 0:
                below = toeplitz
                continue
            product = lax.dot_general(
                jnp.concatenate([toeplitz, below], axis=1),
                windows,
                (((1,), (1,)), ((), ())),
                preferred_element_type=F32,
            )
            if d > 1:
                product = jnp.where(column >= d - 1, pltpu.roll(product, d - 1, 1), 0.0)
            total = total + product
        turned_back = total.T
        result[pl.ds(c, blocks, stride=each), :] = jnp.concatenate(
            [turned_back[:blocks], turned_back[blocks:]], axis=1
        )
        return carry

    lax.fori_loop(0, each, channel, 0)
    out_ref[...] = result[...].reshape(blocks, each, size).astype(BF16)


def mix_kernel(back_ref, q_ref, halo_ref, taps_ref, gated_ref, bias_ref, mixed_ref, rounded_ref, squares_ref, padded):
    rows, channels = q_ref.shape
    query = featured(q_ref, halo_ref[0:2, :], taps_ref, 0, padded)
    long_conv = back_ref[...].astype(F32).reshape(channels, rows).T
    mixed = query * (long_conv + bias_ref[...] * gated_ref[...])
    mixed_ref[...] = mixed
    rounded_ref[...] = mixed.astype(BF16)
    sums = jnp.sum(mixed * mixed, axis=1, keepdims=True)
    squares_ref[...] = jnp.broadcast_to(sums, (rows, rows)).T[0:1, :]


def norm_kernel(total, squares_ref, mixed_ref, gain_ref, out_ref):
    rows = mixed_ref.shape[0]
    squares = jnp.sum(squares_ref[...], axis=0)
    scale = lax.rsqrt(squares / total + EPS)
    scale = jnp.broadcast_to(scale, (rows, rows)).T[:, 0:1]
    out_ref[...] = (mixed_ref[...] * scale * gain_ref[...]).astype(BF16)


def shards(q_proj, k_proj, v_proj, feat_filter, long_filter, skip_bias, norm_gain):
    rows, channels = q_proj.shape
    taps = feat_filter.shape[1]
    groups = lax.axis_size("seq")
    columns = lax.axis_size("ch")
    each = channels // groups
    tail = jnp.concatenate([a[rows - (taps - 1) :, :] for a in (q_proj, k_proj, v_proj)], axis=0)
    halo = lax.ppermute(tail, "seq", [(i, i + 1) for i in range(groups - 1)])
    padded = pltpu.VMEM((rows + 8, channels), F32)
    sent, gated = pl.pallas_call(
        before_kernel,
        out_shape=(
            jax.ShapeDtypeStruct((groups, 2 * each, rows), BF16),
            jax.ShapeDtypeStruct((rows, channels), F32),
        ),
        in_specs=[VMEM] * 5,
        out_specs=(VMEM, VMEM),
        scratch_shapes=[padded],
        name="before",
    )(k_proj, v_proj, halo, feat_filter, long_filter)
    got = lax.all_to_all(sent, "seq", split_axis=0, concat_axis=0, tiled=True)
    scratch = pltpu.VMEM((groups * each, rows), F32)
    conv = pl.pallas_call(
        conv_kernel,
        out_shape=jax.ShapeDtypeStruct((groups, each, rows), BF16),
        in_specs=[VMEM],
        out_specs=VMEM,
        scratch_shapes=[scratch, scratch, scratch],
        name="conv",
    )(got)
    back = lax.all_to_all(conv, "seq", split_axis=0, concat_axis=0, tiled=True)
    mixed, rounded, squares = pl.pallas_call(
        mix_kernel,
        out_shape=(
            jax.ShapeDtypeStruct((rows, channels), F32),
            jax.ShapeDtypeStruct((rows, channels), BF16),
            jax.ShapeDtypeStruct((1, rows), F32),
        ),
        in_specs=[VMEM] * 6,
        out_specs=(VMEM, VMEM, VMEM),
        scratch_shapes=[padded],
        name="mix",
    )(back, q_proj, halo, feat_filter, gated, skip_bias.reshape(1, channels))
    squares = lax.all_gather(squares, "ch")
    normed = pl.pallas_call(
        lambda *refs: norm_kernel(float(columns * channels), *refs),
        out_shape=jax.ShapeDtypeStruct((rows, channels), BF16),
        in_specs=[VMEM] * 3,
        out_specs=VMEM,
        name="norm",
    )(squares, mixed, norm_gain.reshape(1, channels))
    return (rounded, normed)


def solution(mesh):
    return jax.shard_map(
        shards,
        mesh=mesh,
        in_specs=(
            P("seq", "ch"),
            P("seq", "ch"),
            P("seq", "ch"),
            P(None, None, "ch"),
            P("seq", "ch"),
            P("ch"),
            P("ch"),
        ),
        out_specs=(P("seq", "ch"), P("seq", "ch")),
        check_vma=False,
    )
```

```python
import jax
import jax.numpy as jnp
from jax import lax
from jax.experimental import pallas as pl
from jax.experimental.pallas import tpu as pltpu
from jax.sharding import PartitionSpec as P

EPS = 1e-05
F32 = jnp.float32
BF16 = jnp.bfloat16
VMEM = pl.BlockSpec(memory_space=pltpu.VMEM)
PARAMS = pltpu.CompilerParams(vmem_limit_bytes=16 * 2**20)
STEP = 32
SPAN = 4


def tail_kernel(q_ref, k_ref, v_ref, out_ref):
    ends = [ref[...].astype(F32)[-2:] for ref in (q_ref, k_ref, v_ref)]
    out_ref[...] = jnp.concatenate(ends, axis=0).astype(BF16)


def featured(stream_ref, halo, taps_ref, stream, padded):
    rows = stream_ref.shape[0]
    block = stream_ref[...].astype(F32)
    padded[8:, :] = block
    padded[6:8, :] = halo.astype(F32)
    out = taps_ref[stream, 0:1, :] * block
    out = out + taps_ref[stream, 1:2, :] * padded[7 : 7 + rows, :]
    return out + taps_ref[stream, 2:3, :] * padded[6 : 6 + rows, :]


def early_kernel(filter_ref, bias_ref, gain_ref, taps_ref, kept_bias_ref, kept_gain_ref):
    rows = filter_ref.shape[0]
    groups, each, _ = taps_ref.shape
    down = lax.broadcasted_iota(jnp.int32, (rows, rows), 0)
    across = lax.broadcasted_iota(jnp.int32, (rows, rows), 1)
    backwards = (down + across == rows - 1).astype(BF16)
    taps = jnp.dot(backwards, filter_ref[...].astype(BF16), preferred_element_type=F32)
    taps_ref[...] = taps.T.reshape(groups, each, rows)
    kept_bias_ref[...] = bias_ref[...]
    kept_gain_ref[...] = gain_ref[...]


def before_kernel(k_ref, v_ref, halo_ref, taps_ref, filter_ref, bias_ref, sent_ref, direct_ref, padded):
    rows, channels = k_ref.shape
    groups = sent_ref.shape[0]
    key = featured(k_ref, halo_ref[2:4, :], taps_ref, 1, padded)
    value = featured(v_ref, halo_ref[4:6, :], taps_ref, 2, padded)
    gated = key * value
    direct_ref[...] = bias_ref[...] * gated
    signal = gated.T.reshape(groups, channels // groups, rows)
    sent_ref[...] = jnp.concatenate([signal, filter_ref[...]], axis=1).astype(BF16)


def conv_kernel(got_ref, out_ref, signal, taps, result, *toeplitz_refs):
    blocks, both, size = got_ref.shape
    each = both // 2
    step = STEP
    phases = size // step
    span = SPAN
    reach = span * size
    products = blocks // span
    pair = size // blocks
    got = got_ref[...].astype(F32)
    signal[...] = got[:, :each, :].reshape(blocks * each, size)
    taps[...] = got[:, each:, :].reshape(blocks * each, size)
    row = lax.broadcasted_iota(jnp.int32, (step, size), 0)
    lane = lax.broadcasted_iota(jnp.int32, (step, size), 1)
    own = lane < row + (size + 1 - step)
    column = lane % blocks
    token_column = lax.broadcasted_iota(jnp.int32, (size, size), 1) % blocks
    left = lax.broadcasted_iota(jnp.int32, (reach, size), 1) < blocks

    def windows_of(c):
        now = signal[pl.ds(c, blocks, stride=each), :]
        now = jnp.concatenate([now] * pair, axis=0).T
        past = [now]
        for i in range(1, span + 1):
            past.append(jnp.where(token_column >= i, pltpu.roll(now, i, 1), 0.0))
        past = jnp.concatenate(past[::-1], axis=0)
        halves = []
        for w in range(0, phases, 2):
            start = step * w + step
            halves.append(jnp.where(left, past[start : start + reach], past[start + step : start + step + reach]))
        return jnp.concatenate(halves, axis=1).astype(BF16)

    def fill(c, toeplitz_ref):
        before = jnp.zeros((step, size), F32)
        for d in range(blocks):
            spread = jnp.broadcast_to(taps[pl.ds(each * d + c, 1), :], (step, size))
            turned = pltpu.roll(spread, size + 1 - step, 1, stride=1, stride_axis=0)
            g, back = divmod(d, span)
            at = size * (span - 1 - back)
            toeplitz_ref[step * g : step * g + step, at : at + size] = jnp.where(own, turned, before).astype(BF16)
            before = turned

    def finish(c, toeplitz_ref, windows):
        totals = [jnp.zeros((step, size), F32) for _ in range(phases // 2)]
        rows = toeplitz_ref.shape[0] // 2
        for part in range(2):
            product = jnp.dot(toeplitz_ref[rows * part : rows * part + rows, :], windows, preferred_element_type=F32)
            for i in range(products // 2):
                moved = span * (products // 2 * part + i)
                for h in range(phases // 2):
                    term = product[step * i : step * i + step, size * h : size * h + size]
                    if moved:
                        term = jnp.where(column >= moved, pltpu.roll(term, moved, 1), 0.0)
                    totals[h] = totals[h] + term
        turned_back = jnp.concatenate(totals, axis=1).T
        result[pl.ds(c, blocks, stride=each), :] = jnp.concatenate(
            [turned_back[blocks * w : blocks * w + blocks] for w in range(phases)], axis=1
        )

    def channels(i, carry):
        several = len(toeplitz_refs)
        windows = []
        for k in range(several):
            windows.append(windows_of(several * i + k))
            fill(several * i + k, toeplitz_refs[k])
        for k in range(several):
            finish(several * i + k, toeplitz_refs[k], windows[k])
        return carry

    lax.fori_loop(0, each // len(toeplitz_refs), channels, 0)
    out_ref[...] = result[...].reshape(blocks, each, size).astype(BF16)


def mix_kernel(back_ref, q_ref, halo_ref, taps_ref, direct_ref, mixed_ref, rounded_ref, squares_ref, padded):
    rows, channels = q_ref.shape
    query = featured(q_ref, halo_ref[0:2, :], taps_ref, 0, padded)
    long_conv = back_ref[...].astype(F32).reshape(channels, rows).T
    mixed = query * (long_conv + direct_ref[...])
    mixed_ref[...] = mixed
    rounded_ref[...] = mixed.astype(BF16)
    sums = jnp.sum(mixed * mixed, axis=1, keepdims=True)
    squares_ref[...] = jnp.broadcast_to(sums, (rows, rows)).T[0:1, :]


def norm_kernel(total, squares_ref, mixed_ref, gain_ref, out_ref):
    rows = mixed_ref.shape[0]
    squares = jnp.sum(squares_ref[...], axis=0)
    scale = lax.rsqrt(squares / total + EPS)
    scale = jnp.broadcast_to(scale, (rows, rows)).T[:, 0:1]
    out_ref[...] = (mixed_ref[...] * scale * gain_ref[...]).astype(BF16)


def shards(q_proj, k_proj, v_proj, feat_filter, long_filter, skip_bias, norm_gain):
    rows, channels = q_proj.shape
    taps = feat_filter.shape[1]
    groups = lax.axis_size("seq")
    columns = lax.axis_size("ch")
    each = channels // groups
    last = pl.BlockSpec((16, channels), lambda i: (rows // 16 - 1, 0))
    tail = pl.pallas_call(
        tail_kernel,
        grid=(1,),
        out_shape=jax.ShapeDtypeStruct((3 * (taps - 1), channels), BF16),
        in_specs=[last] * 3,
        out_specs=pl.BlockSpec((3 * (taps - 1), channels), lambda i: (0, 0)),
        compiler_params=pltpu.CompilerParams(vmem_limit_bytes=60 * 2**20),
        name="tail",
    )(q_proj, k_proj, v_proj)
    halo = lax.ppermute(tail, "seq", [(i, i + 1) for i in range(groups - 1)])
    padded = pltpu.VMEM((rows + 8, channels), F32)
    row = jax.ShapeDtypeStruct((1, channels), F32)
    kept_filter, kept_bias, kept_gain = pl.pallas_call(
        early_kernel,
        out_shape=(jax.ShapeDtypeStruct((groups, each, rows), F32), row, row),
        in_specs=[VMEM] * 3,
        out_specs=(VMEM,) * 3,
        cost_estimate=pl.CostEstimate(flops=2 * rows * rows * channels, bytes_accessed=8 * rows * channels, transcendentals=0),
        compiler_params=PARAMS,
        name="early",
    )(long_filter, skip_bias.reshape(1, channels), norm_gain.reshape(1, channels))
    sent, direct = pl.pallas_call(
        before_kernel,
        out_shape=(
            jax.ShapeDtypeStruct((groups, 2 * each, rows), BF16),
            jax.ShapeDtypeStruct((rows, channels), F32),
        ),
        in_specs=[VMEM] * 6,
        out_specs=(VMEM, VMEM),
        scratch_shapes=[padded],
        compiler_params=PARAMS,
        name="before",
    )(k_proj, v_proj, halo, feat_filter, kept_filter, kept_bias)
    got = lax.all_to_all(sent, "seq", split_axis=0, concat_axis=0, tiled=True)
    scratch = pltpu.VMEM((groups * each, rows), F32)
    conv = pl.pallas_call(
        conv_kernel,
        out_shape=jax.ShapeDtypeStruct((groups, each, rows), BF16),
        in_specs=[VMEM],
        out_specs=VMEM,
        scratch_shapes=[scratch] * 3 + [pltpu.VMEM((STEP * groups // SPAN, SPAN * rows), BF16)] * 2,
        compiler_params=PARAMS,
        name="conv",
    )(got)
    back = lax.all_to_all(conv, "seq", split_axis=0, concat_axis=0, tiled=True)
    mixed, rounded, squares = pl.pallas_call(
        mix_kernel,
        out_shape=(
            jax.ShapeDtypeStruct((rows, channels), F32),
            jax.ShapeDtypeStruct((rows, channels), BF16),
            jax.ShapeDtypeStruct((1, rows), F32),
        ),
        in_specs=[VMEM] * 5,
        out_specs=(VMEM, VMEM, VMEM),
        scratch_shapes=[padded],
        compiler_params=PARAMS,
        name="mix",
    )(back, q_proj, halo, feat_filter, direct)
    squares = lax.all_gather(squares, "ch")
    normed = pl.pallas_call(
        lambda *refs: norm_kernel(float(columns * channels), *refs),
        out_shape=jax.ShapeDtypeStruct((rows, channels), BF16),
        in_specs=[VMEM] * 3,
        out_specs=VMEM,
        compiler_params=PARAMS,
        name="norm",
    )(squares, mixed, kept_gain)
    return (rounded, normed)


def solution(mesh):
    return jax.shard_map(
        shards,
        mesh=mesh,
        in_specs=(
            P("seq", "ch"),
            P("seq", "ch"),
            P("seq", "ch"),
            P(None, None, "ch"),
            P("seq", "ch"),
            P("ch"),
            P("ch"),
        ),
        out_specs=(P("seq", "ch"), P("seq", "ch")),
        check_vma=False,
    )
```

```python
import jax
import jax.numpy as jnp
from jax import lax
from jax.experimental import pallas as pl
from jax.experimental.pallas import tpu as pltpu
from jax.sharding import PartitionSpec as P

EPS = 1e-05
F32 = jnp.float32
BF16 = jnp.bfloat16
VMEM = pl.BlockSpec(memory_space=pltpu.VMEM)
HBM = pl.BlockSpec(memory_space=pltpu.HBM)
PARAMS = pltpu.CompilerParams(vmem_limit_bytes=16 * 2**20)
STEP = 32
SPAN = 4


def shift_down(block, count):
    return jnp.concatenate([jnp.zeros((count, block.shape[1]), block.dtype), block[:-count]], axis=0)


def inside(stream_ref, taps_ref, stream, padded):
    rows = stream_ref.shape[0]
    block = stream_ref[...].astype(F32)
    padded[8:, :] = block
    padded[6:8, :] = jnp.zeros((2, block.shape[1]), F32)
    out = taps_ref[stream, 0:1, :] * block
    out = out + taps_ref[stream, 1:2, :] * padded[7 : 7 + rows, :]
    return out + taps_ref[stream, 2:3, :] * padded[6 : 6 + rows, :]


def into_next(stream_ref, taps_ref, stream):
    last = stream_ref[stream_ref.shape[0] - 16 :, :].astype(F32)[14:]
    first = taps_ref[stream, 1:2, :] * last[1:] + taps_ref[stream, 2:3, :] * last[:1]
    return [first, taps_ref[stream, 2:3, :] * last[1:]]


def before_kernel(*refs):
    sources, (sent_ref, kept_gain_ref, padded, *kept, sems) = refs[:7], refs[7:]
    loads = [pltpu.make_async_copy(a, b, sems.at[i]) for i, (a, b) in enumerate(zip(sources, kept, strict=True))]
    for load in loads:
        load.start()
    q_ref, k_ref, v_ref, taps_ref, filter_ref, bias_ref, gain_ref = kept
    for load in loads:
        load.wait()
    rows, channels = k_ref.shape
    groups = sent_ref.shape[0]
    each = channels // groups
    key = inside(k_ref, taps_ref, 1, padded)
    value = inside(v_ref, taps_ref, 2, padded)
    signal = (key * value).T.reshape(groups, each, rows)
    down = lax.broadcasted_iota(jnp.int32, (rows, rows), 0)
    across = lax.broadcasted_iota(jnp.int32, (rows, rows), 1)
    backwards = (down + across == rows - 1).astype(BF16)
    taps = jnp.dot(backwards, filter_ref[...].astype(BF16), preferred_element_type=F32)
    taps = taps.T.reshape(groups, each, rows)
    start = q_ref[0:16, :].astype(F32)[0:2]
    first = taps_ref[0, 0:1, :] * start
    second = taps_ref[0, 1:2, :] * start[0:1]
    high = bias_ref[...].astype(BF16).astype(F32)
    middle = (bias_ref[...] - high).astype(BF16).astype(F32)
    low = bias_ref[...] - high - middle
    edge = [key[0:2], value[0:2], first[0:1], first[1:2] + second, jnp.zeros((2, channels), F32)]
    for stream, ref in ((1, k_ref), (2, v_ref), (0, q_ref)):
        edge += into_next(ref, taps_ref, stream)
    edge += [jnp.zeros((2, channels), F32), high, middle, low, jnp.zeros((rows - 19, channels), F32)]
    edge = jnp.concatenate(edge, axis=0).T.reshape(groups, each, rows)
    sent_ref[...] = jnp.concatenate([signal, taps, edge], axis=1).astype(BF16)
    kept_gain_ref[...] = gain_ref[...]


def conv_kernel(got_ref, out_ref, signal, taps, edges, result, *toeplitz_refs):
    blocks, kinds, size = got_ref.shape
    each = kinds // 3
    step = STEP
    phases = size // step
    span = SPAN
    reach = span * size
    products = blocks // span
    pair = size // blocks
    got = got_ref[...].astype(F32)
    signal[...] = got[:, :each, :].reshape(blocks * each, size)
    taps[...] = got[:, each : 2 * each, :].reshape(blocks * each, size)
    edge = got[:, 2 * each :, :].reshape(blocks * each, size)
    edge = edge + pltpu.roll(shift_down(edge, each), size - 8, 1)
    place = lax.broadcasted_iota(jnp.int32, edge.shape, 1)
    signal[...] = jnp.where(place < 2, edge * pltpu.roll(edge, size - 2, 1), signal[...])
    edges[...] = edge
    row = lax.broadcasted_iota(jnp.int32, (step, size), 0)
    lane = lax.broadcasted_iota(jnp.int32, (step, size), 1)
    own = lane < row + (size + 1 - step)
    column = lane % blocks
    place = lax.broadcasted_iota(jnp.int32, (blocks, size), 1)
    start = place < 2
    parts = (place[0:1, :] >= 16) & (place[0:1, :] < 19)
    token_column = lax.broadcasted_iota(jnp.int32, (size, size), 1) % blocks
    left = lax.broadcasted_iota(jnp.int32, (reach, size), 1) < blocks

    def windows_of(c):
        now = signal[pl.ds(c, blocks, stride=each), :]
        now = jnp.concatenate([now] * pair, axis=0).T
        past = [now]
        for i in range(1, span + 1):
            past.append(jnp.where(token_column >= i, pltpu.roll(now, i, 1), 0.0))
        past = jnp.concatenate(past[::-1], axis=0)
        halves = []
        for w in range(0, phases, 2):
            start = step * w + step
            halves.append(jnp.where(left, past[start : start + reach], past[start + step : start + step + reach]))
        return jnp.concatenate(halves, axis=1).astype(BF16)

    def fill(c, toeplitz_ref):
        before = jnp.zeros((step, size), F32)
        for d in range(blocks):
            spread = jnp.broadcast_to(taps[pl.ds(each * d + c, 1), :], (step, size))
            turned = pltpu.roll(spread, size + 1 - step, 1, stride=1, stride_axis=0)
            g, back = divmod(d, span)
            at = size * (span - 1 - back)
            toeplitz_ref[step * g : step * g + step, at : at + size] = jnp.where(own, turned, before).astype(BF16)
            before = turned

    def finish(c, toeplitz_ref, windows):
        totals = [jnp.zeros((step, size), F32) for _ in range(phases // 2)]
        rows = toeplitz_ref.shape[0] // 2
        for part in range(2):
            product = jnp.dot(toeplitz_ref[rows * part : rows * part + rows, :], windows, preferred_element_type=F32)
            for i in range(products // 2):
                moved = span * (products // 2 * part + i)
                for h in range(phases // 2):
                    term = product[step * i : step * i + step, size * h : size * h + size]
                    if moved:
                        term = jnp.where(column >= moved, pltpu.roll(term, moved, 1), 0.0)
                    totals[h] = totals[h] + term
        turned_back = jnp.concatenate(totals, axis=1).T
        turned_back = jnp.concatenate([turned_back[blocks * w : blocks * w + blocks] for w in range(phases)], axis=1)
        edge = edges[pl.ds(c, blocks, stride=each), :]
        direct = jnp.sum(jnp.where(parts, edge[0:1, :], 0.0), axis=1, keepdims=True)
        mixed = turned_back + direct * signal[pl.ds(c, blocks, stride=each), :]
        mixed = mixed * jnp.where(start, pltpu.roll(edge, size - 4, 1), 1.0)
        result[pl.ds(c, blocks, stride=each), :] = mixed

    def channels(i, carry):
        several = len(toeplitz_refs)
        windows = []
        for k in range(several):
            windows.append(windows_of(several * i + k))
            fill(several * i + k, toeplitz_refs[k])
        for k in range(several):
            finish(several * i + k, toeplitz_refs[k], windows[k])
        return carry

    lax.fori_loop(0, each // len(toeplitz_refs), channels, 0)
    out_ref[...] = result[...].reshape(blocks, each, size).astype(BF16)


def mix_kernel(back_ref, q_ref, taps_ref, mixed_ref, rounded_ref, squares_ref, padded):
    rows, channels = q_ref.shape
    query = inside(q_ref, taps_ref, 0, padded)
    back = back_ref[...].astype(F32).reshape(channels, rows).T
    row = lax.broadcasted_iota(jnp.int32, (rows, channels), 0)
    mixed = back * jnp.where(row < 2, 1.0, query)
    mixed_ref[...] = mixed
    rounded_ref[...] = mixed.astype(BF16)
    sums = jnp.sum(mixed * mixed, axis=1, keepdims=True)
    squares_ref[...] = jnp.broadcast_to(sums, (rows, rows)).T[0:1, :]


def norm_kernel(total, squares_ref, mixed_ref, gain_ref, out_ref):
    rows = mixed_ref.shape[0]
    squares = jnp.sum(squares_ref[...], axis=0)
    scale = lax.rsqrt(squares / total + EPS)
    scale = jnp.broadcast_to(scale, (rows, rows)).T[:, 0:1]
    out_ref[...] = (mixed_ref[...] * scale * gain_ref[...]).astype(BF16)


def shards(q_proj, k_proj, v_proj, feat_filter, long_filter, skip_bias, norm_gain):
    rows, channels = q_proj.shape
    groups = lax.axis_size("seq")
    columns = lax.axis_size("ch")
    each = channels // groups
    padded = pltpu.VMEM((rows + 8, channels), F32)
    sources = (q_proj, k_proj, v_proj, feat_filter, long_filter, skip_bias.reshape(1, channels), norm_gain.reshape(1, channels))
    sent, kept_gain = pl.pallas_call(
        before_kernel,
        out_shape=(
            jax.ShapeDtypeStruct((groups, 3 * each, rows), BF16),
            jax.ShapeDtypeStruct((1, channels), F32),
        ),
        in_specs=[HBM] * 7,
        out_specs=(VMEM, VMEM),
        scratch_shapes=[padded] + [pltpu.VMEM(a.shape, a.dtype) for a in sources] + [pltpu.SemaphoreType.DMA((7,))],
        compiler_params=PARAMS,
        name="before",
    )(*(pltpu.with_memory_space_constraint(a, pltpu.HBM) for a in sources))
    got = lax.all_to_all(sent, "seq", split_axis=0, concat_axis=0, tiled=True)
    scratch = pltpu.VMEM((groups * each, rows), F32)
    conv = pl.pallas_call(
        conv_kernel,
        out_shape=jax.ShapeDtypeStruct((groups, each, rows), BF16),
        in_specs=[VMEM],
        out_specs=VMEM,
        scratch_shapes=[scratch] * 4 + [pltpu.VMEM((STEP * groups // SPAN, SPAN * rows), BF16)] * 2,
        compiler_params=PARAMS,
        name="conv",
    )(got)
    back = lax.all_to_all(conv, "seq", split_axis=0, concat_axis=0, tiled=True)
    mixed, rounded, squares = pl.pallas_call(
        mix_kernel,
        out_shape=(
            jax.ShapeDtypeStruct((rows, channels), F32),
            jax.ShapeDtypeStruct((rows, channels), BF16),
            jax.ShapeDtypeStruct((1, rows), F32),
        ),
        in_specs=[VMEM] * 3,
        out_specs=(VMEM, VMEM, VMEM),
        scratch_shapes=[padded],
        compiler_params=PARAMS,
        name="mix",
    )(back, q_proj, feat_filter)
    squares = lax.all_gather(squares, "ch")
    normed = pl.pallas_call(
        lambda *refs: norm_kernel(float(columns * channels), *refs),
        out_shape=jax.ShapeDtypeStruct((rows, channels), BF16),
        in_specs=[VMEM] * 3,
        out_specs=VMEM,
        compiler_params=PARAMS,
        name="norm",
    )(squares, mixed, kept_gain)
    return (rounded, normed)


def solution(mesh):
    return jax.shard_map(
        shards,
        mesh=mesh,
        in_specs=(
            P("seq", "ch"),
            P("seq", "ch"),
            P("seq", "ch"),
            P(None, None, "ch"),
            P("seq", "ch"),
            P("ch"),
            P("ch"),
        ),
        out_specs=(P("seq", "ch"), P("seq", "ch")),
        check_vma=False,
    )
```

```python
import jax
import jax.numpy as jnp
from jax import lax
from jax.experimental import pallas as pl
from jax.experimental.pallas import tpu as pltpu
from jax.sharding import PartitionSpec as P

EPS = 1e-05
F32 = jnp.float32
BF16 = jnp.bfloat16
VMEM = pl.BlockSpec(memory_space=pltpu.VMEM)
HBM = pl.BlockSpec(memory_space=pltpu.HBM)
PARAMS = pltpu.CompilerParams(vmem_limit_bytes=16 * 2**20)
STEP = 32
SPAN = 4
MESSAGE = 18
EDGE = 16


def shift_down(block, count):
    return jnp.concatenate([jnp.zeros((count, block.shape[1]), block.dtype), block[:-count]], axis=0)


def inside(stream_ref, taps_ref, stream, padded):
    rows = stream_ref.shape[0]
    block = stream_ref[...].astype(F32)
    padded[8:, :] = block
    padded[6:8, :] = jnp.zeros((2, block.shape[1]), F32)
    out = taps_ref[stream, 0:1, :] * block
    out = out + taps_ref[stream, 1:2, :] * padded[7 : 7 + rows, :]
    return out + taps_ref[stream, 2:3, :] * padded[6 : 6 + rows, :]


def into_next(stream_ref, taps_ref, stream):
    last = stream_ref[stream_ref.shape[0] - 16 :, :].astype(F32)[14:]
    first = taps_ref[stream, 1:2, :] * last[1:] + taps_ref[stream, 2:3, :] * last[:1]
    return [first, taps_ref[stream, 2:3, :] * last[1:]]


def before_kernel(*refs):
    sources, (sent_ref, kept_gain_ref, padded, edges, *kept, sems) = refs[:7], refs[7:]
    loads = [pltpu.make_async_copy(a, b, sems.at[i]) for i, (a, b) in enumerate(zip(sources, kept, strict=True))]
    for load in loads:
        load.start()
    q_ref, k_ref, v_ref, taps_ref, filter_ref, bias_ref, gain_ref = kept
    for load in loads:
        load.wait()
    rows, channels = k_ref.shape
    groups = sent_ref.shape[0] // MESSAGE
    each = channels // groups
    key = inside(k_ref, taps_ref, 1, padded)
    value = inside(v_ref, taps_ref, 2, padded)
    signal = (key * value).T.reshape(groups, each, rows)
    down = lax.broadcasted_iota(jnp.int32, (rows, rows), 0)
    across = lax.broadcasted_iota(jnp.int32, (rows, rows), 1)
    backwards = (down + across == rows - 1).astype(BF16)
    taps = jnp.dot(backwards, filter_ref[...].astype(BF16), preferred_element_type=F32)
    taps = taps.T.reshape(groups, each, rows)
    start = q_ref[0:16, :].astype(F32)[0:2]
    first = taps_ref[0, 0:1, :] * start
    second = taps_ref[0, 1:2, :] * start[0:1]
    high = bias_ref[...].astype(BF16).astype(F32)
    middle = (bias_ref[...] - high).astype(BF16).astype(F32)
    low = bias_ref[...] - high - middle
    edge = [key[0:2], value[0:2], first[0:1], first[1:2] + second]
    for stream, ref in ((1, k_ref), (2, v_ref), (0, q_ref)):
        edge += into_next(ref, taps_ref, stream)
    edge += [high, middle, low, jnp.zeros((rows - 15, channels), F32)]
    edges[...] = jnp.concatenate(edge, axis=0).T
    edge = edges[pl.ds(0, groups, stride=each), :]
    for c in range(1, each):
        edge = edge + pltpu.roll(edges[pl.ds(c, groups, stride=each), :], EDGE * c, 1)
    blank = jnp.zeros((1, rows), F32)
    messages = []
    for s in range(groups):
        messages += [signal[s], taps[s], edge[s : s + 1], blank]
    sent_ref[...] = jnp.concatenate(messages, axis=0).astype(BF16)
    kept_gain_ref[...] = gain_ref[...]


def conv_kernel(got_ref, out_ref, got, signal, edges, result, *toeplitz_refs):
    blocks, each, size = out_ref.shape
    step = STEP
    phases = size // step
    span = SPAN
    reach = span * size
    products = blocks // span
    pair = size // blocks
    got[...] = got_ref[...].astype(F32)
    row = lax.broadcasted_iota(jnp.int32, (step, size), 0)
    lane = lax.broadcasted_iota(jnp.int32, (step, size), 1)
    own = lane < row + (size + 1 - step)
    column = lane % blocks
    place = lax.broadcasted_iota(jnp.int32, (blocks, size), 1)
    start = place < 2
    parts = (place[0:1, :] >= 12) & (place[0:1, :] < 15)
    packed = got[pl.ds(2 * each, blocks, stride=MESSAGE), :]
    for c in range(each):
        edge = pltpu.roll(packed, size - EDGE * c, 1) if c else packed
        edge = edge + jnp.where(place < 6, pltpu.roll(shift_down(edge, 1), size - 6, 1), 0.0)
        own_tokens = got[pl.ds(c, blocks, stride=MESSAGE), :]
        signal[blocks * c : blocks * c + blocks, :] = jnp.where(start, edge * pltpu.roll(edge, size - 2, 1), own_tokens)
        edges[blocks * c : blocks * c + blocks, :] = edge

    def rows_of(c):
        return pl.ds(pl.multiple_of(blocks * c, blocks), blocks)
    token_column = lax.broadcasted_iota(jnp.int32, (size, size), 1) % blocks
    left = lax.broadcasted_iota(jnp.int32, (reach, size), 1) < blocks

    def windows_of(c):
        now = signal[rows_of(c), :]
        now = jnp.concatenate([now] * pair, axis=0).T
        past = [now]
        for i in range(1, span + 1):
            past.append(jnp.where(token_column >= i, pltpu.roll(now, i, 1), 0.0))
        past = jnp.concatenate(past[::-1], axis=0)
        halves = []
        for w in range(0, phases, 2):
            start = step * w + step
            halves.append(jnp.where(left, past[start : start + reach], past[start + step : start + step + reach]))
        return jnp.concatenate(halves, axis=1).astype(BF16)

    def fill(c, toeplitz_ref):
        before = jnp.zeros((step, size), F32)
        for d in range(blocks):
            spread = jnp.broadcast_to(got[pl.ds(MESSAGE * d + each + c, 1), :], (step, size))
            turned = pltpu.roll(spread, size + 1 - step, 1, stride=1, stride_axis=0)
            g, back = divmod(d, span)
            at = size * (span - 1 - back)
            toeplitz_ref[step * g : step * g + step, at : at + size] = jnp.where(own, turned, before).astype(BF16)
            before = turned

    def finish(c, toeplitz_ref, windows):
        totals = [jnp.zeros((step, size), F32) for _ in range(phases // 2)]
        rows = toeplitz_ref.shape[0] // 2
        for part in range(2):
            product = jnp.dot(toeplitz_ref[rows * part : rows * part + rows, :], windows, preferred_element_type=F32)
            for i in range(products // 2):
                moved = span * (products // 2 * part + i)
                for h in range(phases // 2):
                    term = product[step * i : step * i + step, size * h : size * h + size]
                    if moved:
                        term = jnp.where(column >= moved, pltpu.roll(term, moved, 1), 0.0)
                    totals[h] = totals[h] + term
        turned_back = jnp.concatenate(totals, axis=1).T
        turned_back = jnp.concatenate([turned_back[blocks * w : blocks * w + blocks] for w in range(phases)], axis=1)
        edge = edges[rows_of(c), :]
        direct = jnp.sum(jnp.where(parts, edge[0:1, :], 0.0), axis=1, keepdims=True)
        mixed = turned_back + direct * signal[rows_of(c), :]
        mixed = mixed * jnp.where(start, pltpu.roll(edge, size - 4, 1), 1.0)
        result[pl.ds(c, blocks, stride=each), :] = mixed

    def channels(i, carry):
        several = len(toeplitz_refs)
        windows = []
        for k in range(several):
            windows.append(windows_of(several * i + k))
            fill(several * i + k, toeplitz_refs[k])
        for k in range(several):
            finish(several * i + k, toeplitz_refs[k], windows[k])
        return carry

    lax.fori_loop(0, each // len(toeplitz_refs), channels, 0)
    out_ref[...] = result[...].reshape(blocks, each, size).astype(BF16)


def mix_kernel(back_ref, q_ref, taps_ref, mixed_ref, rounded_ref, squares_ref, padded):
    rows, channels = q_ref.shape
    query = inside(q_ref, taps_ref, 0, padded)
    back = back_ref[...].astype(F32).reshape(channels, rows).T
    row = lax.broadcasted_iota(jnp.int32, (rows, channels), 0)
    mixed = back * jnp.where(row < 2, 1.0, query)
    mixed_ref[...] = mixed
    rounded_ref[...] = mixed.astype(BF16)
    sums = jnp.sum(mixed * mixed, axis=1, keepdims=True)
    squares_ref[...] = jnp.broadcast_to(sums, (rows, rows)).T[0:1, :]


def norm_kernel(total, squares_ref, mixed_ref, gain_ref, out_ref):
    rows = mixed_ref.shape[0]
    squares = jnp.sum(squares_ref[...], axis=0)
    scale = lax.rsqrt(squares / total + EPS)
    scale = jnp.broadcast_to(scale, (rows, rows)).T[:, 0:1]
    out_ref[...] = (mixed_ref[...] * scale * gain_ref[...]).astype(BF16)


def shards(q_proj, k_proj, v_proj, feat_filter, long_filter, skip_bias, norm_gain):
    rows, channels = q_proj.shape
    groups = lax.axis_size("seq")
    columns = lax.axis_size("ch")
    each = channels // groups
    padded = pltpu.VMEM((rows + 8, channels), F32)
    sources = (q_proj, k_proj, v_proj, feat_filter, long_filter, skip_bias.reshape(1, channels), norm_gain.reshape(1, channels))
    sent, kept_gain = pl.pallas_call(
        before_kernel,
        out_shape=(
            jax.ShapeDtypeStruct((groups * MESSAGE, rows), BF16),
            jax.ShapeDtypeStruct((1, channels), F32),
        ),
        in_specs=[HBM] * 7,
        out_specs=(VMEM, VMEM),
        scratch_shapes=[padded, pltpu.VMEM((channels, rows), F32)] + [pltpu.VMEM(a.shape, a.dtype) for a in sources] + [pltpu.SemaphoreType.DMA((7,))],
        compiler_params=PARAMS,
        name="before",
    )(*(pltpu.with_memory_space_constraint(a, pltpu.HBM) for a in sources))
    sent = sent.reshape(groups, MESSAGE // 2, 2, rows)
    got = lax.all_to_all(sent, "seq", split_axis=0, concat_axis=0, tiled=True).reshape(groups * MESSAGE, rows)
    scratch = pltpu.VMEM((groups * each, rows), F32)
    conv = pl.pallas_call(
        conv_kernel,
        out_shape=jax.ShapeDtypeStruct((groups, each, rows), BF16),
        in_specs=[VMEM],
        out_specs=VMEM,
        scratch_shapes=[pltpu.VMEM((groups * MESSAGE, rows), F32)] + [scratch] * 3 + [pltpu.VMEM((STEP * groups // SPAN, SPAN * rows), BF16)] * 2,
        compiler_params=PARAMS,
        name="conv",
    )(got)
    back = lax.all_to_all(conv, "seq", split_axis=0, concat_axis=0, tiled=True)
    mixed, rounded, squares = pl.pallas_call(
        mix_kernel,
        out_shape=(
            jax.ShapeDtypeStruct((rows, channels), F32),
            jax.ShapeDtypeStruct((rows, channels), BF16),
            jax.ShapeDtypeStruct((1, rows), F32),
        ),
        in_specs=[VMEM] * 3,
        out_specs=(VMEM, VMEM, VMEM),
        scratch_shapes=[padded],
        compiler_params=PARAMS,
        name="mix",
    )(back, q_proj, feat_filter)
    squares = lax.all_gather(squares, "ch")
    normed = pl.pallas_call(
        lambda *refs: norm_kernel(float(columns * channels), *refs),
        out_shape=jax.ShapeDtypeStruct((rows, channels), BF16),
        in_specs=[VMEM] * 3,
        out_specs=VMEM,
        compiler_params=PARAMS,
        name="norm",
    )(squares, mixed, kept_gain)
    return (rounded, normed)


def solution(mesh):
    return jax.shard_map(
        shards,
        mesh=mesh,
        in_specs=(
            P("seq", "ch"),
            P("seq", "ch"),
            P("seq", "ch"),
            P(None, None, "ch"),
            P("seq", "ch"),
            P("ch"),
            P("ch"),
        ),
        out_specs=(P("seq", "ch"), P("seq", "ch")),
        check_vma=False,
    )
```

```python
import jax
import jax.numpy as jnp
from jax import lax
from jax.experimental import pallas as pl
from jax.experimental.pallas import tpu as pltpu
from jax.sharding import PartitionSpec as P

EPS = 1e-05
F32 = jnp.float32
BF16 = jnp.bfloat16
VMEM = pl.BlockSpec(memory_space=pltpu.VMEM)
HBM = pl.BlockSpec(memory_space=pltpu.HBM)
PARAMS = pltpu.CompilerParams(vmem_limit_bytes=16 * 2**20)
STEP = 32
SPAN = 4
MESSAGE = 18
EDGE = 16
TOGETHER = 4


def shift_down(block, count):
    return jnp.concatenate([jnp.zeros((count, block.shape[1]), block.dtype), block[:-count]], axis=0)


def inside(stream_ref, taps_ref, stream, padded):
    rows = stream_ref.shape[0]
    block = stream_ref[...].astype(F32)
    padded[8:, :] = block
    padded[6:8, :] = jnp.zeros((2, block.shape[1]), F32)
    out = taps_ref[stream, 0:1, :] * block
    out = out + taps_ref[stream, 1:2, :] * padded[7 : 7 + rows, :]
    return out + taps_ref[stream, 2:3, :] * padded[6 : 6 + rows, :]


def into_next(stream_ref, taps_ref, stream):
    last = stream_ref[stream_ref.shape[0] - 16 :, :].astype(F32)[14:]
    first = taps_ref[stream, 1:2, :] * last[1:] + taps_ref[stream, 2:3, :] * last[:1]
    return [first, taps_ref[stream, 2:3, :] * last[1:]]


def before_kernel(*refs):
    sources, (sent_ref, kept_gain_ref, padded, edges, *kept, sems) = refs[:7], refs[7:]
    loads = [pltpu.make_async_copy(a, b, sems.at[i]) for i, (a, b) in enumerate(zip(sources, kept, strict=True))]
    for load in loads:
        load.start()
    q_ref, k_ref, v_ref, taps_ref, filter_ref, bias_ref, gain_ref = kept
    rows, channels = k_ref.shape
    groups = sent_ref.shape[0] // MESSAGE
    each = channels // groups
    for load in (loads[1], loads[2], loads[3]):
        load.wait()
    key = inside(k_ref, taps_ref, 1, padded)
    value = inside(v_ref, taps_ref, 2, padded)
    signal = (key * value).T.reshape(groups, each, rows)
    down = lax.broadcasted_iota(jnp.int32, (rows, rows), 0)
    across = lax.broadcasted_iota(jnp.int32, (rows, rows), 1)
    backwards = (down + across == rows - 1).astype(BF16)
    loads[4].wait()
    taps = jnp.dot(backwards, filter_ref[...].astype(BF16), preferred_element_type=F32)
    taps = taps.T.reshape(groups, each, rows)
    for load in (loads[0], loads[5], loads[6]):
        load.wait()
    start = q_ref[0:16, :].astype(F32)[0:2]
    first = taps_ref[0, 0:1, :] * start
    second = taps_ref[0, 1:2, :] * start[0:1]
    high = bias_ref[...].astype(BF16).astype(F32)
    middle = (bias_ref[...] - high).astype(BF16).astype(F32)
    low = bias_ref[...] - high - middle
    edge = [key[0:2], value[0:2], first[0:1], first[1:2] + second]
    for stream, ref in ((1, k_ref), (2, v_ref), (0, q_ref)):
        edge += into_next(ref, taps_ref, stream)
    edge += [high, middle, low, jnp.zeros((rows - 15, channels), F32)]
    edges[...] = jnp.concatenate(edge, axis=0).T
    edge = edges[pl.ds(0, groups, stride=each), :]
    for c in range(1, each):
        edge = edge + pltpu.roll(edges[pl.ds(c, groups, stride=each), :], EDGE * c, 1)
    blank = jnp.zeros((1, rows), F32)
    messages = []
    for s in range(groups):
        messages += [signal[s], taps[s], edge[s : s + 1], blank]
    sent_ref[...] = jnp.concatenate(messages, axis=0).astype(BF16)
    kept_gain_ref[...] = gain_ref[...]


def conv_kernel(got_ref, out_ref, got, signal, edges, result, phased, *buffers):
    blocks, each, size = out_ref.shape
    step = STEP
    phases = size // step
    steps = blocks * phases
    several = len(buffers) // 2
    windows_refs, toeplitz_refs = buffers[:several], buffers[several:]
    got[...] = got_ref[...].astype(F32)
    lane = lax.broadcasted_iota(jnp.int32, (blocks, size), 1)
    own = lax.broadcasted_iota(jnp.int32, (step, size), 1) < lax.broadcasted_iota(jnp.int32, (step, size), 0) + (size + 1 - step)
    start = lane < 2
    parts = (lane[0:1, :] >= 8) & (lane[0:1, :] < 11)
    edge = got[pl.ds(2 * each, blocks, stride=MESSAGE), :]
    edge = edge + jnp.where(lane % EDGE < 6, pltpu.roll(shift_down(edge, 1), size - 6, 1), 0.0)
    first = edge * pltpu.roll(edge, size - 2, 1)
    for c in range(each):
        at = slice(blocks * c, blocks * c + blocks)
        turned = pltpu.roll(first, size - EDGE * c, 1) if c else first
        signal[at, :] = jnp.where(start, turned, got[pl.ds(c, blocks, stride=MESSAGE), :])
        edges[at, :] = pltpu.roll(edge, (2 * size - EDGE * c - 4) % size, 1)
    for windows_ref in windows_refs:
        windows_ref[:16, :] = jnp.zeros((16, size), F32)

    def rows_of(c):
        return pl.ds(pl.multiple_of(blocks * c, blocks), blocks)

    def steps_of(c, windows_ref):
        now = signal[rows_of(c), :]
        for w in range(phases):
            left = size - step * w - step
            if left:
                turned = pltpu.roll(now, left, 1)
                windows_ref[pl.ds(16 + w, blocks, stride=phases), :] = jnp.where(lane < left, shift_down(turned, 1), turned)
            else:
                windows_ref[pl.ds(16 + w, blocks, stride=phases), :] = now

    def fill(c, toeplitz_ref):
        before = jnp.zeros((step, size), BF16)
        for d in range(blocks):
            spread = jnp.broadcast_to(got[pl.ds(MESSAGE * d + each + c, 1), :], (step, size))
            turned = pltpu.roll(spread, size + 1 - step, 1, stride=1, stride_axis=0).astype(BF16)
            g, back = divmod(d, SPAN)
            at = size * (SPAN - 1 - back)
            toeplitz_ref[step * g : step * g + step, at : at + size] = jnp.where(own, turned, before)
            before = turned

    def later(rows, count):
        return jnp.concatenate([jnp.zeros((count, size), F32), rows[: rows.shape[0] - count]], axis=0) if count else rows

    def finish(c, windows_ref, toeplitz_ref):
        starts = [16 - phases * (SPAN - 1 - u) for u in range(SPAN)]
        windows = jnp.concatenate([windows_ref[a : a + steps, :] for a in starts], axis=1).astype(BF16)
        move = phases * SPAN
        group = size // step
        totals = jnp.zeros((steps, size), F32)
        wide = 2 * size
        for n in range(toeplitz_ref.shape[0] // wide):
            rows = steps - 2 * n * group * move
            product = lax.dot_general(
                windows[:rows],
                toeplitz_ref[wide * n : wide * n + wide, :],
                (((1,), (1,)), ((), ())),
                preferred_element_type=F32,
            )
            for half in range(2):
                count = (2 * n + half) * group * move
                part = product[: steps - count, size * half : size * half + size]
                totals = totals + (jnp.concatenate([jnp.zeros((count, size), F32), part], axis=0) if count else part)
        together = totals
        for i in range(1, group):
            together = together + later(pltpu.roll(totals, size - step * i, 1), move * i)
        phased[...] = together
        out = phased[pl.ds(0, blocks, stride=phases), :]
        for w in range(1, phases):
            out = jnp.where(lane < step * w, out, pltpu.roll(phased[pl.ds(w, blocks, stride=phases), :], step * w, 1))
        edge = edges[rows_of(c), :]
        direct = jnp.sum(jnp.where(parts, edge[0:1, :], 0.0), axis=1, keepdims=True)
        mixed = out + direct * signal[rows_of(c), :]
        result[pl.ds(c, blocks, stride=each), :] = mixed * jnp.where(start, edge, 1.0)

    def channels(i, carry):
        for k in range(several):
            steps_of(several * i + k, windows_refs[k])
            fill(several * i + k, toeplitz_refs[k])
        for k in range(several):
            finish(several * i + k, windows_refs[k], toeplitz_refs[k])
        return carry

    lax.fori_loop(0, each // several, channels, 0)
    out_ref[...] = result[...].reshape(blocks, each, size).astype(BF16)


def mix_kernel(back_ref, q_ref, taps_ref, mixed_ref, squares_ref, padded):
    rows, channels = q_ref.shape
    query = inside(q_ref, taps_ref, 0, padded)
    back = back_ref[...].astype(F32).reshape(channels, rows).T
    row = lax.broadcasted_iota(jnp.int32, (rows, channels), 0)
    mixed = back * jnp.where(row < 2, 1.0, query)
    mixed_ref[...] = mixed
    sums = jnp.sum(mixed * mixed, axis=1, keepdims=True)
    squares_ref[...] = jnp.broadcast_to(sums, (rows, rows)).T[0:1, :]


def norm_kernel(total, squares_ref, mixed_ref, gain_ref, rounded_ref, out_ref):
    rows = mixed_ref.shape[0]
    rounded_ref[...] = mixed_ref[...].astype(BF16)
    squares = jnp.sum(squares_ref[...], axis=0)
    scale = lax.rsqrt(squares / total + EPS)
    scale = jnp.broadcast_to(scale, (rows, rows)).T[:, 0:1]
    out_ref[...] = (mixed_ref[...] * scale * gain_ref[...]).astype(BF16)


def shards(q_proj, k_proj, v_proj, feat_filter, long_filter, skip_bias, norm_gain):
    rows, channels = q_proj.shape
    groups = lax.axis_size("seq")
    columns = lax.axis_size("ch")
    each = channels // groups
    padded = pltpu.VMEM((rows + 8, channels), F32)
    sources = (q_proj, k_proj, v_proj, feat_filter, long_filter, skip_bias.reshape(1, channels), norm_gain.reshape(1, channels))
    sent, kept_gain = pl.pallas_call(
        before_kernel,
        out_shape=(
            jax.ShapeDtypeStruct((groups * MESSAGE, rows), BF16),
            jax.ShapeDtypeStruct((1, channels), F32),
        ),
        in_specs=[HBM] * 7,
        out_specs=(VMEM, VMEM),
        scratch_shapes=[padded, pltpu.VMEM((channels, rows), F32)] + [pltpu.VMEM(a.shape, a.dtype) for a in sources] + [pltpu.SemaphoreType.DMA((7,))],
        compiler_params=PARAMS,
        name="before",
    )(*(pltpu.with_memory_space_constraint(a, pltpu.HBM) for a in sources))
    sent = sent.reshape(groups, MESSAGE // 2, 2, rows)
    got = lax.all_to_all(sent, "seq", split_axis=0, concat_axis=0, tiled=True).reshape(groups * MESSAGE, rows)
    scratch = pltpu.VMEM((groups * each, rows), F32)
    conv = pl.pallas_call(
        conv_kernel,
        out_shape=jax.ShapeDtypeStruct((groups, each, rows), BF16),
        in_specs=[VMEM],
        out_specs=VMEM,
        scratch_shapes=[pltpu.VMEM((groups * MESSAGE, rows), F32)]
        + [scratch] * 3
        + [pltpu.VMEM((groups * rows // STEP, rows), F32)]
        + [pltpu.VMEM((groups * rows // STEP + 16, rows), F32)] * TOGETHER
        + [pltpu.VMEM((STEP * groups // SPAN, SPAN * rows), BF16)] * TOGETHER,
        compiler_params=PARAMS,
        name="conv",
    )(got)
    back = lax.all_to_all(conv, "seq", split_axis=0, concat_axis=0, tiled=True)
    mixed, squares = pl.pallas_call(
        mix_kernel,
        out_shape=(
            jax.ShapeDtypeStruct((rows, channels), F32),
            jax.ShapeDtypeStruct((1, rows), F32),
        ),
        in_specs=[VMEM] * 3,
        out_specs=(VMEM, VMEM),
        scratch_shapes=[padded],
        compiler_params=PARAMS,
        name="mix",
    )(back, q_proj, feat_filter)
    squares = lax.all_gather(squares, "ch")
    rounded, normed = pl.pallas_call(
        lambda *refs: norm_kernel(float(columns * channels), *refs),
        out_shape=(jax.ShapeDtypeStruct((rows, channels), BF16),) * 2,
        in_specs=[VMEM] * 3,
        out_specs=(VMEM, VMEM),
        compiler_params=PARAMS,
        name="norm",
    )(squares, mixed, kept_gain)
    return (rounded, normed)


def solution(mesh):
    return jax.shard_map(
        shards,
        mesh=mesh,
        in_specs=(
            P("seq", "ch"),
            P("seq", "ch"),
            P("seq", "ch"),
            P(None, None, "ch"),
            P("seq", "ch"),
            P("ch"),
            P("ch"),
        ),
        out_specs=(P("seq", "ch"), P("seq", "ch")),
        check_vma=False,
    )
```

```python
import jax
import jax.numpy as jnp
from jax import lax
from jax.experimental import pallas as pl
from jax.experimental.pallas import tpu as pltpu
from jax.sharding import PartitionSpec as P

EPS = 1e-05
F32 = jnp.float32
BF16 = jnp.bfloat16
VMEM = pl.BlockSpec(memory_space=pltpu.VMEM)
HBM = pl.BlockSpec(memory_space=pltpu.HBM)
PARAMS = pltpu.CompilerParams(vmem_limit_bytes=16 * 2**20)
STEP = 32
SPAN = 4
MESSAGE = 18
EDGE = 16
TOGETHER = 4


def shift_down(block, count):
    return jnp.concatenate([jnp.zeros((count, block.shape[1]), block.dtype), block[:-count]], axis=0)


def inside(stream_ref, taps_ref, stream, padded):
    rows = stream_ref.shape[0]
    block = stream_ref[...].astype(F32)
    padded[8:, :] = block
    padded[6:8, :] = jnp.zeros((2, block.shape[1]), F32)
    out = taps_ref[stream, 0:1, :] * block
    out = out + taps_ref[stream, 1:2, :] * padded[7 : 7 + rows, :]
    return out + taps_ref[stream, 2:3, :] * padded[6 : 6 + rows, :]


def into_next(stream_ref, taps_ref, stream):
    last = stream_ref[stream_ref.shape[0] - 16 :, :].astype(F32)[14:]
    first = taps_ref[stream, 1:2, :] * last[1:] + taps_ref[stream, 2:3, :] * last[:1]
    return [first, taps_ref[stream, 2:3, :] * last[1:]]


def before_kernel(*refs):
    sources, (sent_ref, kept_gain_ref, padded, edges, *kept, sems) = refs[:7], refs[7:]
    loads = [pltpu.make_async_copy(a, b, sems.at[i]) for i, (a, b) in enumerate(zip(sources, kept, strict=True))]
    for load in loads:
        load.start()
    q_ref, k_ref, v_ref, taps_ref, filter_ref, bias_ref, gain_ref = kept
    for load in loads:
        load.wait()
    rows, channels = k_ref.shape
    groups = sent_ref.shape[0] // MESSAGE
    each = channels // groups
    key = inside(k_ref, taps_ref, 1, padded)
    value = inside(v_ref, taps_ref, 2, padded)
    signal = (key * value).T.reshape(groups, each, rows)
    down = lax.broadcasted_iota(jnp.int32, (rows, rows), 0)
    across = lax.broadcasted_iota(jnp.int32, (rows, rows), 1)
    backwards = (down + across == rows - 1).astype(BF16)
    taps = jnp.dot(backwards, filter_ref[...].astype(BF16), preferred_element_type=F32)
    taps = taps.T.reshape(groups, each, rows)
    start = q_ref[0:16, :].astype(F32)[0:2]
    first = taps_ref[0, 0:1, :] * start
    second = taps_ref[0, 1:2, :] * start[0:1]
    high = bias_ref[...].astype(BF16).astype(F32)
    middle = (bias_ref[...] - high).astype(BF16).astype(F32)
    low = bias_ref[...] - high - middle
    edge = [key[0:2], value[0:2], first[0:1], first[1:2] + second]
    for stream, ref in ((1, k_ref), (2, v_ref), (0, q_ref)):
        edge += into_next(ref, taps_ref, stream)
    edge += [high, middle, low, jnp.zeros((rows - 15, channels), F32)]
    edges[...] = jnp.concatenate(edge, axis=0).T
    edge = edges[pl.ds(0, groups, stride=each), :]
    for c in range(1, each):
        edge = edge + pltpu.roll(edges[pl.ds(c, groups, stride=each), :], EDGE * c, 1)
    blank = jnp.zeros((1, rows), F32)
    messages = []
    for s in range(groups):
        messages += [signal[s], taps[s], edge[s : s + 1], blank]
    sent_ref[...] = jnp.concatenate(messages, axis=0).astype(BF16)
    kept_gain_ref[...] = gain_ref[...]


def conv_kernel(got_ref, out_ref, got, signal, edges, result, phased, *buffers):
    blocks, each, size = out_ref.shape
    step = STEP
    phases = size // step
    steps = blocks * phases
    several = len(buffers) // 2
    windows_refs, toeplitz_refs = buffers[:several], buffers[several:]
    got[...] = got_ref[...].astype(F32)
    lane = lax.broadcasted_iota(jnp.int32, (blocks, size), 1)
    own = lax.broadcasted_iota(jnp.int32, (step, size), 1) < lax.broadcasted_iota(jnp.int32, (step, size), 0) + (size + 1 - step)
    start = lane < 2
    parts = (lane[0:1, :] >= 8) & (lane[0:1, :] < 11)
    edge = got[pl.ds(2 * each, blocks, stride=MESSAGE), :]
    edge = edge + jnp.where(lane % EDGE < 6, pltpu.roll(shift_down(edge, 1), size - 6, 1), 0.0)
    first = edge * pltpu.roll(edge, size - 2, 1)
    for c in range(each):
        at = slice(blocks * c, blocks * c + blocks)
        turned = pltpu.roll(first, size - EDGE * c, 1) if c else first
        signal[at, :] = jnp.where(start, turned, got[pl.ds(c, blocks, stride=MESSAGE), :])
        edges[at, :] = pltpu.roll(edge, (2 * size - EDGE * c - 4) % size, 1)
    for windows_ref in windows_refs:
        windows_ref[:16, :] = jnp.zeros((16, size), F32)

    def rows_of(c):
        return pl.ds(pl.multiple_of(blocks * c, blocks), blocks)

    def steps_of(c, windows_ref):
        now = signal[rows_of(c), :]
        for w in range(phases):
            left = size - step * w - step
            if left:
                turned = pltpu.roll(now, left, 1)
                windows_ref[pl.ds(16 + w, blocks, stride=phases), :] = jnp.where(lane < left, shift_down(turned, 1), turned)
            else:
                windows_ref[pl.ds(16 + w, blocks, stride=phases), :] = now

    def fill(c, toeplitz_ref):
        before = jnp.zeros((step, size), BF16)
        for d in range(blocks):
            spread = jnp.broadcast_to(got[pl.ds(MESSAGE * d + each + c, 1), :], (step, size))
            turned = pltpu.roll(spread, size + 1 - step, 1, stride=1, stride_axis=0).astype(BF16)
            g, back = divmod(d, SPAN)
            at = size * (SPAN - 1 - back)
            toeplitz_ref[step * g : step * g + step, at : at + size] = jnp.where(own, turned, before)
            before = turned

    def later(rows, count):
        return jnp.concatenate([jnp.zeros((count, size), F32), rows[: rows.shape[0] - count]], axis=0) if count else rows

    def finish(c, windows_ref, toeplitz_ref):
        starts = [16 - phases * (SPAN - 1 - u) for u in range(SPAN)]
        windows = jnp.concatenate([windows_ref[a : a + steps, :] for a in starts], axis=1).astype(BF16)
        move = phases * SPAN
        group = size // step
        totals = jnp.zeros((steps, size), F32)
        wide = 2 * size
        for n in range(toeplitz_ref.shape[0] // wide):
            rows = steps - 2 * n * group * move
            product = lax.dot_general(
                windows[:rows],
                toeplitz_ref[wide * n : wide * n + wide, :],
                (((1,), (1,)), ((), ())),
                preferred_element_type=F32,
            )
            for half in range(2):
                count = (2 * n + half) * group * move
                part = product[: steps - count, size * half : size * half + size]
                totals = totals + (jnp.concatenate([jnp.zeros((count, size), F32), part], axis=0) if count else part)
        together = totals
        for i in range(1, group):
            together = together + later(pltpu.roll(totals, size - step * i, 1), move * i)
        phased[...] = together
        out = phased[pl.ds(0, blocks, stride=phases), :]
        for w in range(1, phases):
            out = jnp.where(lane < step * w, out, pltpu.roll(phased[pl.ds(w, blocks, stride=phases), :], step * w, 1))
        edge = edges[rows_of(c), :]
        direct = jnp.sum(jnp.where(parts, edge[0:1, :], 0.0), axis=1, keepdims=True)
        mixed = out + direct * signal[rows_of(c), :]
        result[pl.ds(c, blocks, stride=each), :] = mixed * jnp.where(start, edge, 1.0)

    def channels(i, carry):
        for k in range(several):
            steps_of(several * i + k, windows_refs[k])
            fill(several * i + k, toeplitz_refs[k])
        for k in range(several):
            finish(several * i + k, windows_refs[k], toeplitz_refs[k])
        return carry

    lax.fori_loop(0, each // several, channels, 0)
    out_ref[...] = result[...].reshape(blocks, each, size).astype(BF16)


def mix_kernel(back_ref, q_ref, taps_ref, mixed_ref, squares_ref, padded):
    rows, channels = q_ref.shape
    query = inside(q_ref, taps_ref, 0, padded)
    back = back_ref[...].astype(F32).reshape(channels, rows).T
    row = lax.broadcasted_iota(jnp.int32, (rows, channels), 0)
    mixed = back * jnp.where(row < 2, 1.0, query)
    mixed_ref[...] = mixed
    sums = jnp.sum(mixed * mixed, axis=1, keepdims=True)
    squares_ref[...] = jnp.broadcast_to(sums, (rows, rows)).T[: squares_ref.shape[0]]


def norm_kernel(total, squares_ref, mixed_ref, gain_ref, rounded_ref, out_ref):
    rows = mixed_ref.shape[0]
    rounded_ref[...] = mixed_ref[...].astype(BF16)
    squares = jnp.sum(squares_ref[...], axis=0, keepdims=True)
    scale = lax.rsqrt(squares / total + EPS)
    scale = jnp.broadcast_to(scale, (rows, rows)).T[:, 0:1]
    out_ref[...] = (mixed_ref[...] * scale * gain_ref[...]).astype(BF16)


def shards(q_proj, k_proj, v_proj, feat_filter, long_filter, skip_bias, norm_gain):
    rows, channels = q_proj.shape
    groups = lax.axis_size("seq")
    columns = lax.axis_size("ch")
    each = channels // groups
    padded = pltpu.VMEM((rows + 8, channels), F32)
    sources = (q_proj, k_proj, v_proj, feat_filter, long_filter, skip_bias.reshape(1, channels), norm_gain.reshape(1, channels))
    sent, kept_gain = pl.pallas_call(
        before_kernel,
        out_shape=(
            jax.ShapeDtypeStruct((groups * MESSAGE, rows), BF16),
            jax.ShapeDtypeStruct((1, channels), F32),
        ),
        in_specs=[HBM] * 7,
        out_specs=(VMEM, VMEM),
        scratch_shapes=[padded, pltpu.VMEM((channels, rows), F32)] + [pltpu.VMEM(a.shape, a.dtype) for a in sources] + [pltpu.SemaphoreType.DMA((7,))],
        compiler_params=PARAMS,
        name="before",
    )(*(pltpu.with_memory_space_constraint(a, pltpu.HBM) for a in sources))
    sent = sent.reshape(groups, MESSAGE // 2, 2, rows)
    got = lax.all_to_all(sent, "seq", split_axis=0, concat_axis=0, tiled=True).reshape(groups * MESSAGE, rows)
    scratch = pltpu.VMEM((groups * each, rows), F32)
    conv = pl.pallas_call(
        conv_kernel,
        out_shape=jax.ShapeDtypeStruct((groups, each, rows), BF16),
        in_specs=[VMEM],
        out_specs=VMEM,
        scratch_shapes=[pltpu.VMEM((groups * MESSAGE, rows), F32)]
        + [scratch] * 3
        + [pltpu.VMEM((groups * rows // STEP, rows), F32)]
        + [pltpu.VMEM((groups * rows // STEP + 16, rows), F32)] * TOGETHER
        + [pltpu.VMEM((STEP * groups // SPAN, SPAN * rows), BF16)] * TOGETHER,
        compiler_params=PARAMS,
        name="conv",
    )(got)
    back = lax.all_to_all(conv, "seq", split_axis=0, concat_axis=0, tiled=True)
    mixed, squares = pl.pallas_call(
        mix_kernel,
        out_shape=(
            jax.ShapeDtypeStruct((rows, channels), F32),
            jax.ShapeDtypeStruct((columns, rows), F32),
        ),
        in_specs=[VMEM] * 3,
        out_specs=(VMEM, VMEM),
        scratch_shapes=[padded],
        compiler_params=PARAMS,
        name="mix",
    )(back, q_proj, feat_filter)
    squares = lax.all_to_all(squares, "ch", split_axis=0, concat_axis=0, tiled=True)
    rounded, normed = pl.pallas_call(
        lambda *refs: norm_kernel(float(columns * channels), *refs),
        out_shape=(jax.ShapeDtypeStruct((rows, channels), BF16),) * 2,
        in_specs=[VMEM] * 3,
        out_specs=(VMEM, VMEM),
        compiler_params=PARAMS,
        name="norm",
    )(squares, mixed, kept_gain)
    return (rounded, normed)


def solution(mesh):
    return jax.shard_map(
        shards,
        mesh=mesh,
        in_specs=(
            P("seq", "ch"),
            P("seq", "ch"),
            P("seq", "ch"),
            P(None, None, "ch"),
            P("seq", "ch"),
            P("ch"),
            P("ch"),
        ),
        out_specs=(P("seq", "ch"), P("seq", "ch")),
        check_vma=False,
    )
```

```python
import jax
import jax.numpy as jnp
from jax import lax
from jax.experimental import pallas as pl
from jax.experimental.pallas import tpu as pltpu
from jax.sharding import PartitionSpec as P

EPS = 1e-05
F32 = jnp.float32
BF16 = jnp.bfloat16
VMEM = pl.BlockSpec(memory_space=pltpu.VMEM)
HBM = pl.BlockSpec(memory_space=pltpu.HBM)
PARAMS = pltpu.CompilerParams(vmem_limit_bytes=16 * 2**20)
STEP = 32
SPAN = 2
MESSAGE = 18
EDGE = 16
TOGETHER = 8


def shift_down(block, count):
    return jnp.concatenate([jnp.zeros((count, block.shape[1]), block.dtype), block[:-count]], axis=0)


def inside(stream_ref, taps_ref, stream, padded):
    rows = stream_ref.shape[0]
    block = stream_ref[...].astype(F32)
    padded[8:, :] = block
    padded[6:8, :] = jnp.zeros((2, block.shape[1]), F32)
    out = taps_ref[stream, 0:1, :] * block
    out = out + taps_ref[stream, 1:2, :] * padded[7 : 7 + rows, :]
    return out + taps_ref[stream, 2:3, :] * padded[6 : 6 + rows, :]


def into_next(stream_ref, taps_ref, stream):
    last = stream_ref[stream_ref.shape[0] - 16 :, :].astype(F32)[14:]
    first = taps_ref[stream, 1:2, :] * last[1:] + taps_ref[stream, 2:3, :] * last[:1]
    return [first, taps_ref[stream, 2:3, :] * last[1:]]


def before_kernel(*refs):
    sources, (sent_ref, kept_gain_ref, padded, edges, *kept, sems) = refs[:7], refs[7:]
    loads = [pltpu.make_async_copy(a, b, sems.at[i]) for i, (a, b) in enumerate(zip(sources, kept, strict=True))]
    for load in loads:
        load.start()
    q_ref, k_ref, v_ref, taps_ref, filter_ref, bias_ref, gain_ref = kept
    for load in loads:
        load.wait()
    rows, channels = k_ref.shape
    groups = sent_ref.shape[0] // MESSAGE
    each = channels // groups
    key = inside(k_ref, taps_ref, 1, padded)
    value = inside(v_ref, taps_ref, 2, padded)
    signal = (key * value).T.reshape(groups, each, rows)
    down = lax.broadcasted_iota(jnp.int32, (rows, rows), 0)
    across = lax.broadcasted_iota(jnp.int32, (rows, rows), 1)
    backwards = (down + across == rows - 1).astype(BF16)
    taps = jnp.dot(backwards, filter_ref[...].astype(BF16), preferred_element_type=F32)
    taps = taps.T.reshape(groups, each, rows)
    start = q_ref[0:16, :].astype(F32)[0:2]
    first = taps_ref[0, 0:1, :] * start
    second = taps_ref[0, 1:2, :] * start[0:1]
    high = bias_ref[...].astype(BF16).astype(F32)
    middle = (bias_ref[...] - high).astype(BF16).astype(F32)
    low = bias_ref[...] - high - middle
    edge = [key[0:2], value[0:2], first[0:1], first[1:2] + second]
    for stream, ref in ((1, k_ref), (2, v_ref), (0, q_ref)):
        edge += into_next(ref, taps_ref, stream)
    edge += [high, middle, low, jnp.zeros((rows - 15, channels), F32)]
    edges[...] = jnp.concatenate(edge, axis=0).T
    edge = edges[pl.ds(0, groups, stride=each), :]
    for c in range(1, each):
        edge = edge + pltpu.roll(edges[pl.ds(c, groups, stride=each), :], EDGE * c, 1)
    blank = jnp.zeros((1, rows), F32)
    messages = []
    for s in range(groups):
        messages += [signal[s], taps[s], edge[s : s + 1], blank]
    sent_ref[...] = jnp.concatenate(messages, axis=0).astype(BF16)
    kept_gain_ref[...] = gain_ref[...]


def conv_kernel(got_ref, out_ref, got, signal, edges, result, phased, *buffers):
    blocks, each, size = out_ref.shape
    step = STEP
    phases = size // step
    steps = blocks * phases
    several = len(buffers) // 2
    windows_refs, toeplitz_refs = buffers[:several], buffers[several:]
    got[...] = got_ref[...].astype(F32)
    lane = lax.broadcasted_iota(jnp.int32, (blocks, size), 1)
    own = lax.broadcasted_iota(jnp.int32, (step, size), 1) < lax.broadcasted_iota(jnp.int32, (step, size), 0) + (size + 1 - step)
    start = lane < 2
    parts = (lane[0:1, :] >= 8) & (lane[0:1, :] < 11)
    edge = got[pl.ds(2 * each, blocks, stride=MESSAGE), :]
    edge = edge + jnp.where(lane % EDGE < 6, pltpu.roll(shift_down(edge, 1), size - 6, 1), 0.0)
    first = edge * pltpu.roll(edge, size - 2, 1)
    for c in range(each):
        at = slice(blocks * c, blocks * c + blocks)
        turned = pltpu.roll(first, size - EDGE * c, 1) if c else first
        signal[at, :] = jnp.where(start, turned, got[pl.ds(c, blocks, stride=MESSAGE), :])
        edges[at, :] = pltpu.roll(edge, (2 * size - EDGE * c - 4) % size, 1)
    for windows_ref in windows_refs:
        windows_ref[:16, :] = jnp.zeros((16, size), F32)

    phased[: phased.shape[0] - steps, :] = jnp.zeros((phased.shape[0] - steps, size), F32)

    def rows_of(c):
        return pl.ds(pl.multiple_of(blocks * c, blocks), blocks)

    def steps_of(c, windows_ref):
        now = signal[rows_of(c), :]
        for w in range(phases):
            left = size - step * w - step
            if left:
                turned = pltpu.roll(now, left, 1)
                windows_ref[pl.ds(16 + w, blocks, stride=phases), :] = jnp.where(lane < left, shift_down(turned, 1), turned)
            else:
                windows_ref[pl.ds(16 + w, blocks, stride=phases), :] = now

    def fill(c, toeplitz_ref):
        before = jnp.zeros((step, size), BF16)
        for d in range(blocks):
            spread = jnp.broadcast_to(got[pl.ds(MESSAGE * d + each + c, 1), :], (step, size))
            turned = pltpu.roll(spread, size + 1 - step, 1, stride=1, stride_axis=0).astype(BF16)
            g, back = divmod(d, SPAN)
            at = size * (SPAN - 1 - back)
            toeplitz_ref[step * g : step * g + step, at : at + size] = jnp.where(own, turned, before)
            before = turned

    def finish(c, windows_ref, toeplitz_ref):
        starts = [16 - phases * (SPAN - 1 - u) for u in range(SPAN)]
        windows = jnp.concatenate([windows_ref[a : a + steps, :] for a in starts], axis=1).astype(BF16)
        move = phases * SPAN
        group = size // step
        totals = jnp.zeros((steps, size), F32)
        wide = 2 * size
        for n in range(toeplitz_ref.shape[0] // wide):
            rows = steps - 2 * n * group * move
            product = lax.dot_general(
                windows[:rows],
                toeplitz_ref[wide * n : wide * n + wide, :],
                (((1,), (1,)), ((), ())),
                preferred_element_type=F32,
            )
            for half in range(2):
                count = (2 * n + half) * group * move
                part = product[: steps - count, size * half : size * half + size]
                totals = totals + (jnp.concatenate([jnp.zeros((count, size), F32), part], axis=0) if count else part)
        ahead = move * (group - 1)
        phased[ahead:, :] = totals
        out = None
        for r in range(phases):
            mine = None
            for i in range(group):
                source = phased[pl.ds(ahead - move * i + (i + r) % phases, blocks, stride=phases), :]
                mine = jnp.where(lane < step * i, mine, source) if i else source
            out = out + pltpu.roll(mine, step * r, 1) if r else mine
        edge = edges[rows_of(c), :]
        direct = jnp.sum(jnp.where(parts, edge[0:1, :], 0.0), axis=1, keepdims=True)
        mixed = out + direct * signal[rows_of(c), :]
        result[pl.ds(c, blocks, stride=each), :] = mixed * jnp.where(start, edge, 1.0)

    def channels(i, carry):
        for k in range(several):
            steps_of(several * i + k, windows_refs[k])
            fill(several * i + k, toeplitz_refs[k])
        for k in range(several):
            finish(several * i + k, windows_refs[k], toeplitz_refs[k])
        return carry

    lax.fori_loop(0, each // several, channels, 0)
    out_ref[...] = result[...].reshape(blocks, each, size).astype(BF16)


def mix_kernel(back_ref, q_ref, taps_ref, mixed_ref, squares_ref, padded):
    rows, channels = q_ref.shape
    query = inside(q_ref, taps_ref, 0, padded)
    back = back_ref[...].astype(F32).reshape(channels, rows).T
    row = lax.broadcasted_iota(jnp.int32, (rows, channels), 0)
    mixed = back * jnp.where(row < 2, 1.0, query)
    mixed_ref[...] = mixed
    sums = jnp.sum(mixed * mixed, axis=1, keepdims=True)
    squares_ref[...] = jnp.broadcast_to(sums, (rows, rows)).T[: squares_ref.shape[0]]


def norm_kernel(total, squares_ref, mixed_ref, gain_ref, rounded_ref, out_ref):
    rows = mixed_ref.shape[0]
    rounded_ref[...] = mixed_ref[...].astype(BF16)
    squares = jnp.sum(squares_ref[...], axis=0, keepdims=True)
    scale = lax.rsqrt(squares / total + EPS)
    scale = jnp.broadcast_to(scale, (rows, rows)).T[:, 0:1]
    out_ref[...] = (mixed_ref[...] * scale * gain_ref[...]).astype(BF16)


def shards(q_proj, k_proj, v_proj, feat_filter, long_filter, skip_bias, norm_gain):
    rows, channels = q_proj.shape
    groups = lax.axis_size("seq")
    columns = lax.axis_size("ch")
    each = channels // groups
    padded = pltpu.VMEM((rows + 8, channels), F32)
    sources = (q_proj, k_proj, v_proj, feat_filter, long_filter, skip_bias.reshape(1, channels), norm_gain.reshape(1, channels))
    sent, kept_gain = pl.pallas_call(
        before_kernel,
        out_shape=(
            jax.ShapeDtypeStruct((groups * MESSAGE, rows), BF16),
            jax.ShapeDtypeStruct((1, channels), F32),
        ),
        in_specs=[HBM] * 7,
        out_specs=(VMEM, VMEM),
        scratch_shapes=[padded, pltpu.VMEM((channels, rows), F32)] + [pltpu.VMEM(a.shape, a.dtype) for a in sources] + [pltpu.SemaphoreType.DMA((7,))],
        compiler_params=PARAMS,
        name="before",
    )(*(pltpu.with_memory_space_constraint(a, pltpu.HBM) for a in sources))
    sent = sent.reshape(groups, MESSAGE // 2, 2, rows)
    got = lax.all_to_all(sent, "seq", split_axis=0, concat_axis=0, tiled=True).reshape(groups * MESSAGE, rows)
    scratch = pltpu.VMEM((groups * each, rows), F32)
    conv = pl.pallas_call(
        conv_kernel,
        out_shape=jax.ShapeDtypeStruct((groups, each, rows), BF16),
        in_specs=[VMEM],
        out_specs=VMEM,
        scratch_shapes=[pltpu.VMEM((groups * MESSAGE, rows), F32)]
        + [scratch] * 3
        + [pltpu.VMEM((groups * rows // STEP + (rows // STEP - 1) * SPAN * rows // STEP, rows), F32)]
        + [pltpu.VMEM((groups * rows // STEP + 16, rows), F32)] * TOGETHER
        + [pltpu.VMEM((STEP * groups // SPAN, SPAN * rows), BF16)] * TOGETHER,
        compiler_params=PARAMS,
        name="conv",
    )(got)
    back = lax.all_to_all(conv, "seq", split_axis=0, concat_axis=0, tiled=True)
    mixed, squares = pl.pallas_call(
        mix_kernel,
        out_shape=(
            jax.ShapeDtypeStruct((rows, channels), F32),
            jax.ShapeDtypeStruct((columns, rows), F32),
        ),
        in_specs=[VMEM] * 3,
        out_specs=(VMEM, VMEM),
        scratch_shapes=[padded],
        compiler_params=PARAMS,
        name="mix",
    )(back, q_proj, feat_filter)
    squares = lax.all_to_all(squares, "ch", split_axis=0, concat_axis=0, tiled=True)
    rounded, normed = pl.pallas_call(
        lambda *refs: norm_kernel(float(columns * channels), *refs),
        out_shape=(jax.ShapeDtypeStruct((rows, channels), BF16),) * 2,
        in_specs=[VMEM] * 3,
        out_specs=(VMEM, VMEM),
        compiler_params=PARAMS,
        name="norm",
    )(squares, mixed, kept_gain)
    return (rounded, normed)


def solution(mesh):
    return jax.shard_map(
        shards,
        mesh=mesh,
        in_specs=(
            P("seq", "ch"),
            P("seq", "ch"),
            P("seq", "ch"),
            P(None, None, "ch"),
            P("seq", "ch"),
            P("ch"),
            P("ch"),
        ),
        out_specs=(P("seq", "ch"), P("seq", "ch")),
        check_vma=False,
    )
```

```python
import jax
import jax.numpy as jnp
from jax import lax
from jax.experimental import pallas as pl
from jax.experimental.pallas import tpu as pltpu
from jax.sharding import PartitionSpec as P

EPS = 1e-05
F32 = jnp.float32
BF16 = jnp.bfloat16
VMEM = pl.BlockSpec(memory_space=pltpu.VMEM)
HBM = pl.BlockSpec(memory_space=pltpu.HBM)
PARAMS = pltpu.CompilerParams(vmem_limit_bytes=16 * 2**20)
STEP = 32
SPAN = 2
MESSAGE = 18
EDGE = 16
TOGETHER = 8


def shift_down(block, count):
    return jnp.concatenate([jnp.zeros((count, block.shape[1]), block.dtype), block[:-count]], axis=0)


def inside(stream_ref, taps_ref, stream, padded):
    rows = stream_ref.shape[0]
    block = stream_ref[...].astype(F32)
    padded[8:, :] = block
    padded[6:8, :] = jnp.zeros((2, block.shape[1]), F32)
    out = taps_ref[stream, 0:1, :] * block
    out = out + taps_ref[stream, 1:2, :] * padded[7 : 7 + rows, :]
    return out + taps_ref[stream, 2:3, :] * padded[6 : 6 + rows, :]


def into_next(stream_ref, taps_ref, stream):
    last = stream_ref[stream_ref.shape[0] - 16 :, :].astype(F32)[14:]
    first = taps_ref[stream, 1:2, :] * last[1:] + taps_ref[stream, 2:3, :] * last[:1]
    return [first, taps_ref[stream, 2:3, :] * last[1:]]


def before_kernel(*refs):
    sources, (sent_ref, kept_gain_ref, padded, edges, *kept, sems) = refs[:7], refs[7:]
    loads = [pltpu.make_async_copy(a, b, sems.at[i]) for i, (a, b) in enumerate(zip(sources, kept, strict=True))]
    for load in loads:
        load.start()
    q_ref, k_ref, v_ref, taps_ref, filter_ref, bias_ref, gain_ref = kept
    for load in loads:
        load.wait()
    rows, channels = k_ref.shape
    groups = sent_ref.shape[0] // MESSAGE
    each = channels // groups
    key = inside(k_ref, taps_ref, 1, padded)
    value = inside(v_ref, taps_ref, 2, padded)
    signal = (key * value).T.reshape(groups, each, rows)
    down = lax.broadcasted_iota(jnp.int32, (rows, rows), 0)
    across = lax.broadcasted_iota(jnp.int32, (rows, rows), 1)
    backwards = (down + across == rows - 1).astype(BF16)
    taps = jnp.dot(backwards, filter_ref[...].astype(BF16), preferred_element_type=F32)
    taps = taps.T.reshape(groups, each, rows)
    start = q_ref[0:16, :].astype(F32)[0:2]
    first = taps_ref[0, 0:1, :] * start
    second = taps_ref[0, 1:2, :] * start[0:1]
    high = bias_ref[...].astype(BF16).astype(F32)
    middle = (bias_ref[...] - high).astype(BF16).astype(F32)
    low = bias_ref[...] - high - middle
    edge = [key[0:2], value[0:2], first[0:1], first[1:2] + second]
    for stream, ref in ((1, k_ref), (2, v_ref), (0, q_ref)):
        edge += into_next(ref, taps_ref, stream)
    edge += [high, middle, low, jnp.zeros((rows - 15, channels), F32)]
    edges[...] = jnp.concatenate(edge, axis=0).T
    edge = edges[pl.ds(0, groups, stride=each), :]
    for c in range(1, each):
        edge = edge + pltpu.roll(edges[pl.ds(c, groups, stride=each), :], EDGE * c, 1)
    rest = edge - edge.astype(BF16).astype(F32)
    messages = []
    for s in range(groups):
        messages += [signal[s], taps[s], edge[s : s + 1], rest[s : s + 1]]
    sent_ref[...] = jnp.concatenate(messages, axis=0).astype(BF16)
    kept_gain_ref[...] = gain_ref[...]


def conv_kernel(got_ref, out_ref, got, signal, edges, result, phased, *buffers):
    blocks, each, size = out_ref.shape
    step = STEP
    phases = size // step
    steps = blocks * phases
    several = len(buffers) // 2
    windows_refs, toeplitz_refs = buffers[:several], buffers[several:]
    got[...] = got_ref[...].astype(F32)
    lane = lax.broadcasted_iota(jnp.int32, (blocks, size), 1)
    own = lax.broadcasted_iota(jnp.int32, (step, size), 1) < lax.broadcasted_iota(jnp.int32, (step, size), 0) + (size + 1 - step)
    start = lane < 2
    parts = (lane[0:1, :] >= 8) & (lane[0:1, :] < 11)
    edge = got[pl.ds(2 * each, blocks, stride=MESSAGE), :] + got[pl.ds(2 * each + 1, blocks, stride=MESSAGE), :]
    edge = edge + jnp.where(lane % EDGE < 6, pltpu.roll(shift_down(edge, 1), size - 6, 1), 0.0)
    first = edge * pltpu.roll(edge, size - 2, 1)
    for c in range(each):
        at = slice(blocks * c, blocks * c + blocks)
        turned = pltpu.roll(first, size - EDGE * c, 1) if c else first
        signal[at, :] = jnp.where(start, turned, got[pl.ds(c, blocks, stride=MESSAGE), :])
        edges[at, :] = pltpu.roll(edge, (2 * size - EDGE * c - 4) % size, 1)
    for windows_ref in windows_refs:
        windows_ref[:16, :] = jnp.zeros((16, size), F32)

    phased[: phased.shape[0] - steps, :] = jnp.zeros((phased.shape[0] - steps, size), F32)

    def rows_of(c):
        return pl.ds(pl.multiple_of(blocks * c, blocks), blocks)

    def steps_of(c, windows_ref):
        now = signal[rows_of(c), :]
        for w in range(phases):
            left = size - step * w - step
            if left:
                turned = pltpu.roll(now, left, 1)
                windows_ref[pl.ds(16 + w, blocks, stride=phases), :] = jnp.where(lane < left, shift_down(turned, 1), turned)
            else:
                windows_ref[pl.ds(16 + w, blocks, stride=phases), :] = now

    def fill(c, toeplitz_ref):
        before = jnp.zeros((step, size), BF16)
        for d in range(blocks):
            spread = jnp.broadcast_to(got[pl.ds(MESSAGE * d + each + c, 1), :], (step, size))
            turned = pltpu.roll(spread, size + 1 - step, 1, stride=1, stride_axis=0).astype(BF16)
            g, back = divmod(d, SPAN)
            at = size * (SPAN - 1 - back)
            toeplitz_ref[step * g : step * g + step, at : at + size] = jnp.where(own, turned, before)
            before = turned

    def finish(c, windows_ref, toeplitz_ref):
        starts = [16 - phases * (SPAN - 1 - u) for u in range(SPAN)]
        windows = jnp.concatenate([windows_ref[a : a + steps, :] for a in starts], axis=1).astype(BF16)
        move = phases * SPAN
        group = size // step
        totals = jnp.zeros((steps, size), F32)
        wide = 2 * size
        for n in range(toeplitz_ref.shape[0] // wide):
            rows = steps - 2 * n * group * move
            product = lax.dot_general(
                windows[:rows],
                toeplitz_ref[wide * n : wide * n + wide, :],
                (((1,), (1,)), ((), ())),
                preferred_element_type=F32,
            )
            for half in range(2):
                count = (2 * n + half) * group * move
                part = product[: steps - count, size * half : size * half + size]
                totals = totals + (jnp.concatenate([jnp.zeros((count, size), F32), part], axis=0) if count else part)
        ahead = move * (group - 1)
        phased[ahead:, :] = totals
        out = None
        for r in range(phases):
            mine = None
            for i in range(group):
                source = phased[pl.ds(ahead - move * i + (i + r) % phases, blocks, stride=phases), :]
                mine = jnp.where(lane < step * i, mine, source) if i else source
            out = out + pltpu.roll(mine, step * r, 1) if r else mine
        edge = edges[rows_of(c), :]
        direct = jnp.sum(jnp.where(parts, edge[0:1, :], 0.0), axis=1, keepdims=True)
        mixed = out + direct * signal[rows_of(c), :]
        result[pl.ds(c, blocks, stride=each), :] = mixed * jnp.where(start, edge, 1.0)

    def channels(i, carry):
        for k in range(several):
            steps_of(several * i + k, windows_refs[k])
            fill(several * i + k, toeplitz_refs[k])
        for k in range(several):
            finish(several * i + k, windows_refs[k], toeplitz_refs[k])
        return carry

    lax.fori_loop(0, each // several, channels, 0)
    out_ref[...] = result[...].reshape(blocks, each, size).astype(BF16)


def mix_kernel(back_ref, q_ref, taps_ref, mixed_ref, squares_ref, padded):
    rows, channels = q_ref.shape
    query = inside(q_ref, taps_ref, 0, padded)
    back = back_ref[...].astype(F32).reshape(channels, rows).T
    row = lax.broadcasted_iota(jnp.int32, (rows, channels), 0)
    mixed = back * jnp.where(row < 2, 1.0, query)
    mixed_ref[...] = mixed
    sums = jnp.sum(mixed * mixed, axis=1, keepdims=True)
    squares_ref[...] = jnp.broadcast_to(sums, (rows, rows)).T[: squares_ref.shape[0]]


def norm_kernel(total, squares_ref, mixed_ref, gain_ref, rounded_ref, out_ref):
    rows = mixed_ref.shape[0]
    rounded_ref[...] = mixed_ref[...].astype(BF16)
    squares = jnp.sum(squares_ref[...], axis=0, keepdims=True)
    scale = lax.rsqrt(squares / total + EPS)
    scale = jnp.broadcast_to(scale, (rows, rows)).T[:, 0:1]
    out_ref[...] = (mixed_ref[...] * scale * gain_ref[...]).astype(BF16)


def shards(q_proj, k_proj, v_proj, feat_filter, long_filter, skip_bias, norm_gain):
    rows, channels = q_proj.shape
    groups = lax.axis_size("seq")
    columns = lax.axis_size("ch")
    each = channels // groups
    padded = pltpu.VMEM((rows + 8, channels), F32)
    sources = (q_proj, k_proj, v_proj, feat_filter, long_filter, skip_bias.reshape(1, channels), norm_gain.reshape(1, channels))
    sent, kept_gain = pl.pallas_call(
        before_kernel,
        out_shape=(
            jax.ShapeDtypeStruct((groups * MESSAGE, rows), BF16),
            jax.ShapeDtypeStruct((1, channels), F32),
        ),
        in_specs=[HBM] * 7,
        out_specs=(VMEM, VMEM),
        scratch_shapes=[padded, pltpu.VMEM((channels, rows), F32)] + [pltpu.VMEM(a.shape, a.dtype) for a in sources] + [pltpu.SemaphoreType.DMA((7,))],
        compiler_params=PARAMS,
        name="before",
    )(*(pltpu.with_memory_space_constraint(a, pltpu.HBM) for a in sources))
    sent = sent.reshape(groups, MESSAGE // 2, 2, rows)
    got = lax.all_to_all(sent, "seq", split_axis=0, concat_axis=0, tiled=True).reshape(groups * MESSAGE, rows)
    scratch = pltpu.VMEM((groups * each, rows), F32)
    conv = pl.pallas_call(
        conv_kernel,
        out_shape=jax.ShapeDtypeStruct((groups, each, rows), BF16),
        in_specs=[VMEM],
        out_specs=VMEM,
        scratch_shapes=[pltpu.VMEM((groups * MESSAGE, rows), F32)]
        + [scratch] * 3
        + [pltpu.VMEM((groups * rows // STEP + (rows // STEP - 1) * SPAN * rows // STEP, rows), F32)]
        + [pltpu.VMEM((groups * rows // STEP + 16, rows), F32)] * TOGETHER
        + [pltpu.VMEM((STEP * groups // SPAN, SPAN * rows), BF16)] * TOGETHER,
        compiler_params=PARAMS,
        name="conv",
    )(got)
    back = lax.all_to_all(conv, "seq", split_axis=0, concat_axis=0, tiled=True)
    mixed, squares = pl.pallas_call(
        mix_kernel,
        out_shape=(
            jax.ShapeDtypeStruct((rows, channels), F32),
            jax.ShapeDtypeStruct((columns, rows), F32),
        ),
        in_specs=[VMEM] * 3,
        out_specs=(VMEM, VMEM),
        scratch_shapes=[padded],
        compiler_params=PARAMS,
        name="mix",
    )(back, q_proj, feat_filter)
    squares = lax.all_to_all(squares, "ch", split_axis=0, concat_axis=0, tiled=True)
    rounded, normed = pl.pallas_call(
        lambda *refs: norm_kernel(float(columns * channels), *refs),
        out_shape=(jax.ShapeDtypeStruct((rows, channels), BF16),) * 2,
        in_specs=[VMEM] * 3,
        out_specs=(VMEM, VMEM),
        compiler_params=PARAMS,
        name="norm",
    )(squares, mixed, kept_gain)
    return (rounded, normed)


def solution(mesh):
    return jax.shard_map(
        shards,
        mesh=mesh,
        in_specs=(
            P("seq", "ch"),
            P("seq", "ch"),
            P("seq", "ch"),
            P(None, None, "ch"),
            P("seq", "ch"),
            P("ch"),
            P("ch"),
        ),
        out_specs=(P("seq", "ch"), P("seq", "ch")),
        check_vma=False,
    )
```

```python
import jax
import jax.numpy as jnp
from jax import lax
from jax.experimental import pallas as pl
from jax.experimental.pallas import tpu as pltpu
from jax.sharding import PartitionSpec as P

EPS = 1e-05
F32 = jnp.float32
BF16 = jnp.bfloat16
VMEM = pl.BlockSpec(memory_space=pltpu.VMEM)
HBM = pl.BlockSpec(memory_space=pltpu.HBM)
PARAMS = pltpu.CompilerParams(vmem_limit_bytes=16 * 2**20)
STEP = 32
SPAN = 2
MESSAGE = 18
EDGE = 16
TOGETHER = 8


def shift_down(block, count):
    return jnp.concatenate([jnp.zeros((count, block.shape[1]), block.dtype), block[:-count]], axis=0)


def inside(stream_ref, taps_ref, stream, padded):
    rows = stream_ref.shape[0]
    block = stream_ref[...].astype(F32)
    padded[8:, :] = block
    padded[6:8, :] = jnp.zeros((2, block.shape[1]), F32)
    out = taps_ref[stream, 0:1, :] * block
    out = out + taps_ref[stream, 1:2, :] * padded[7 : 7 + rows, :]
    return out + taps_ref[stream, 2:3, :] * padded[6 : 6 + rows, :]


def into_next(stream_ref, taps_ref, stream):
    last = stream_ref[stream_ref.shape[0] - 16 :, :].astype(F32)[14:]
    first = taps_ref[stream, 1:2, :] * last[1:] + taps_ref[stream, 2:3, :] * last[:1]
    return [first, taps_ref[stream, 2:3, :] * last[1:]]


def before_kernel(*refs):
    sources, (sent_ref, kept_gain_ref, padded, edges, *kept, sems) = refs[:7], refs[7:]
    pairs = list(zip(sources[1:], kept[1:], strict=True))
    for at in (pl.ds(0, 16), pl.ds(kept[0].shape[0] - 16, 16)):
        pairs.append((sources[0].at[at], kept[0].at[at]))
    loads = [pltpu.make_async_copy(a, b, sems.at[i]) for i, (a, b) in enumerate(pairs)]
    for load in loads:
        load.start()
    q_ref, k_ref, v_ref, taps_ref, filter_ref, bias_ref, gain_ref = kept
    for i in (0, 1, 2, 4, 5, 6, 7):
        loads[i].wait()
    rows, channels = k_ref.shape
    groups = sent_ref.shape[0] // MESSAGE
    each = channels // groups
    key = inside(k_ref, taps_ref, 1, padded)
    value = inside(v_ref, taps_ref, 2, padded)
    signal = (key * value).T.reshape(groups, each, rows)
    down = lax.broadcasted_iota(jnp.int32, (rows, rows), 0)
    across = lax.broadcasted_iota(jnp.int32, (rows, rows), 1)
    backwards = (down + across == rows - 1).astype(BF16)
    loads[3].wait()
    taps = jnp.dot(backwards, filter_ref[...].astype(BF16), preferred_element_type=F32)
    taps = taps.T.reshape(groups, each, rows)
    start = q_ref[0:16, :].astype(F32)[0:2]
    first = taps_ref[0, 0:1, :] * start
    second = taps_ref[0, 1:2, :] * start[0:1]
    high = bias_ref[...].astype(BF16).astype(F32)
    middle = (bias_ref[...] - high).astype(BF16).astype(F32)
    low = bias_ref[...] - high - middle
    edge = [key[0:2], value[0:2], first[0:1], first[1:2] + second]
    for stream, ref in ((1, k_ref), (2, v_ref), (0, q_ref)):
        edge += into_next(ref, taps_ref, stream)
    edge += [high, middle, low, jnp.zeros((rows - 15, channels), F32)]
    edges[...] = jnp.concatenate(edge, axis=0).T
    edge = edges[pl.ds(0, groups, stride=each), :]
    for c in range(1, each):
        edge = edge + pltpu.roll(edges[pl.ds(c, groups, stride=each), :], EDGE * c, 1)
    rest = edge - edge.astype(BF16).astype(F32)
    messages = []
    for s in range(groups):
        messages += [signal[s], taps[s], edge[s : s + 1], rest[s : s + 1]]
    sent_ref[...] = jnp.concatenate(messages, axis=0).astype(BF16)
    kept_gain_ref[...] = gain_ref[...]


def conv_kernel(got_ref, out_ref, got, signal, edges, result, phased, *buffers):
    blocks, each, size = out_ref.shape
    step = STEP
    phases = size // step
    steps = blocks * phases
    several = len(buffers) // 2
    windows_refs, toeplitz_refs = buffers[:several], buffers[several:]
    got[...] = got_ref[...].astype(F32)
    lane = lax.broadcasted_iota(jnp.int32, (blocks, size), 1)
    own = lax.broadcasted_iota(jnp.int32, (step, size), 1) < lax.broadcasted_iota(jnp.int32, (step, size), 0) + (size + 1 - step)
    start = lane < 2
    parts = (lane[0:1, :] >= 8) & (lane[0:1, :] < 11)
    edge = got[pl.ds(2 * each, blocks, stride=MESSAGE), :] + got[pl.ds(2 * each + 1, blocks, stride=MESSAGE), :]
    edge = edge + jnp.where(lane % EDGE < 6, pltpu.roll(shift_down(edge, 1), size - 6, 1), 0.0)
    first = edge * pltpu.roll(edge, size - 2, 1)
    for c in range(each):
        at = slice(blocks * c, blocks * c + blocks)
        turned = pltpu.roll(first, size - EDGE * c, 1) if c else first
        signal[at, :] = jnp.where(start, turned, got[pl.ds(c, blocks, stride=MESSAGE), :])
        edges[at, :] = pltpu.roll(edge, (2 * size - EDGE * c - 4) % size, 1)
    for windows_ref in windows_refs:
        windows_ref[:16, :] = jnp.zeros((16, size), F32)

    phased[: phased.shape[0] - steps, :] = jnp.zeros((phased.shape[0] - steps, size), F32)

    def rows_of(c):
        return pl.ds(pl.multiple_of(blocks * c, blocks), blocks)

    def steps_of(c, windows_ref):
        now = signal[rows_of(c), :]
        for w in range(phases):
            left = size - step * w - step
            if left:
                turned = pltpu.roll(now, left, 1)
                windows_ref[pl.ds(16 + w, blocks, stride=phases), :] = jnp.where(lane < left, shift_down(turned, 1), turned)
            else:
                windows_ref[pl.ds(16 + w, blocks, stride=phases), :] = now

    def fill(c, toeplitz_ref):
        before = jnp.zeros((step, size), BF16)
        for d in range(blocks):
            spread = jnp.broadcast_to(got[pl.ds(MESSAGE * d + each + c, 1), :], (step, size))
            turned = pltpu.roll(spread, size + 1 - step, 1, stride=1, stride_axis=0).astype(BF16)
            g, back = divmod(d, SPAN)
            at = size * (SPAN - 1 - back)
            toeplitz_ref[step * g : step * g + step, at : at + size] = jnp.where(own, turned, before)
            before = turned

    def finish(c, windows_ref, toeplitz_ref):
        starts = [16 - phases * (SPAN - 1 - u) for u in range(SPAN)]
        windows = jnp.concatenate([windows_ref[a : a + steps, :] for a in starts], axis=1).astype(BF16)
        move = phases * SPAN
        group = size // step
        totals = jnp.zeros((steps, size), F32)
        wide = 2 * size
        for n in range(toeplitz_ref.shape[0] // wide):
            rows = steps - 2 * n * group * move
            product = lax.dot_general(
                windows[:rows],
                toeplitz_ref[wide * n : wide * n + wide, :],
                (((1,), (1,)), ((), ())),
                preferred_element_type=F32,
            )
            for half in range(2):
                count = (2 * n + half) * group * move
                part = product[: steps - count, size * half : size * half + size]
                totals = totals + (jnp.concatenate([jnp.zeros((count, size), F32), part], axis=0) if count else part)
        ahead = move * (group - 1)
        phased[ahead:, :] = totals
        out = None
        for r in range(phases):
            mine = None
            for i in range(group):
                source = phased[pl.ds(ahead - move * i + (i + r) % phases, blocks, stride=phases), :]
                mine = jnp.where(lane < step * i, mine, source) if i else source
            out = out + pltpu.roll(mine, step * r, 1) if r else mine
        edge = edges[rows_of(c), :]
        direct = jnp.sum(jnp.where(parts, edge[0:1, :], 0.0), axis=1, keepdims=True)
        mixed = out + direct * signal[rows_of(c), :]
        result[pl.ds(c, blocks, stride=each), :] = mixed * jnp.where(start, edge, 1.0)

    def channels(i, carry):
        for k in range(several):
            steps_of(several * i + k, windows_refs[k])
            fill(several * i + k, toeplitz_refs[k])
        for k in range(several):
            finish(several * i + k, windows_refs[k], toeplitz_refs[k])
        return carry

    lax.fori_loop(0, each // several, channels, 0)
    out_ref[...] = result[...].reshape(blocks, each, size).astype(BF16)


def mix_kernel(back_ref, q_ref, taps_ref, mixed_ref, squares_ref, padded):
    rows, channels = q_ref.shape
    query = inside(q_ref, taps_ref, 0, padded)
    back = back_ref[...].astype(F32).reshape(channels, rows).T
    row = lax.broadcasted_iota(jnp.int32, (rows, channels), 0)
    mixed = back * jnp.where(row < 2, 1.0, query)
    mixed_ref[...] = mixed
    sums = jnp.sum(mixed * mixed, axis=1, keepdims=True)
    squares_ref[...] = jnp.broadcast_to(sums, (rows, rows)).T[: squares_ref.shape[0]]


def norm_kernel(total, squares_ref, mixed_ref, gain_ref, rounded_ref, out_ref):
    rows = mixed_ref.shape[0]
    rounded_ref[...] = mixed_ref[...].astype(BF16)
    squares = jnp.sum(squares_ref[...], axis=0, keepdims=True)
    scale = lax.rsqrt(squares / total + EPS)
    scale = jnp.broadcast_to(scale, (rows, rows)).T[:, 0:1]
    out_ref[...] = (mixed_ref[...] * scale * gain_ref[...]).astype(BF16)


def shards(q_proj, k_proj, v_proj, feat_filter, long_filter, skip_bias, norm_gain):
    rows, channels = q_proj.shape
    groups = lax.axis_size("seq")
    columns = lax.axis_size("ch")
    each = channels // groups
    padded = pltpu.VMEM((rows + 8, channels), F32)
    sources = (q_proj, k_proj, v_proj, feat_filter, long_filter, skip_bias.reshape(1, channels), norm_gain.reshape(1, channels))
    sent, kept_gain = pl.pallas_call(
        before_kernel,
        out_shape=(
            jax.ShapeDtypeStruct((groups * MESSAGE, rows), BF16),
            jax.ShapeDtypeStruct((1, channels), F32),
        ),
        in_specs=[HBM] * 7,
        out_specs=(VMEM, VMEM),
        scratch_shapes=[padded, pltpu.VMEM((channels, rows), F32)] + [pltpu.VMEM(a.shape, a.dtype) for a in sources] + [pltpu.SemaphoreType.DMA((8,))],
        compiler_params=PARAMS,
        name="before",
    )(*(pltpu.with_memory_space_constraint(a, pltpu.HBM) for a in sources))
    sent = sent.reshape(groups, MESSAGE // 2, 2, rows)
    got = lax.all_to_all(sent, "seq", split_axis=0, concat_axis=0, tiled=True).reshape(groups * MESSAGE, rows)
    scratch = pltpu.VMEM((groups * each, rows), F32)
    conv = pl.pallas_call(
        conv_kernel,
        out_shape=jax.ShapeDtypeStruct((groups, each, rows), BF16),
        in_specs=[VMEM],
        out_specs=VMEM,
        scratch_shapes=[pltpu.VMEM((groups * MESSAGE, rows), F32)]
        + [scratch] * 3
        + [pltpu.VMEM((groups * rows // STEP + (rows // STEP - 1) * SPAN * rows // STEP, rows), F32)]
        + [pltpu.VMEM((groups * rows // STEP + 16, rows), F32)] * TOGETHER
        + [pltpu.VMEM((STEP * groups // SPAN, SPAN * rows), BF16)] * TOGETHER,
        compiler_params=PARAMS,
        name="conv",
    )(got)
    back = lax.all_to_all(conv, "seq", split_axis=0, concat_axis=0, tiled=True)
    mixed, squares = pl.pallas_call(
        mix_kernel,
        out_shape=(
            jax.ShapeDtypeStruct((rows, channels), F32),
            jax.ShapeDtypeStruct((columns, rows), F32),
        ),
        in_specs=[VMEM] * 3,
        out_specs=(VMEM, VMEM),
        scratch_shapes=[padded],
        compiler_params=PARAMS,
        name="mix",
    )(back, q_proj, feat_filter)
    squares = lax.all_to_all(squares, "ch", split_axis=0, concat_axis=0, tiled=True)
    rounded, normed = pl.pallas_call(
        lambda *refs: norm_kernel(float(columns * channels), *refs),
        out_shape=(jax.ShapeDtypeStruct((rows, channels), BF16),) * 2,
        in_specs=[VMEM] * 3,
        out_specs=(VMEM, VMEM),
        compiler_params=PARAMS,
        name="norm",
    )(squares, mixed, kept_gain)
    return (rounded, normed)


def solution(mesh):
    return jax.shard_map(
        shards,
        mesh=mesh,
        in_specs=(
            P("seq", "ch"),
            P("seq", "ch"),
            P("seq", "ch"),
            P(None, None, "ch"),
            P("seq", "ch"),
            P("ch"),
            P("ch"),
        ),
        out_specs=(P("seq", "ch"), P("seq", "ch")),
        check_vma=False,
    )
```

```python
import jax
import jax.numpy as jnp
from jax import lax
from jax.experimental import pallas as pl
from jax.experimental.pallas import tpu as pltpu
from jax.sharding import PartitionSpec as P

EPS = 1e-05
F32 = jnp.float32
BF16 = jnp.bfloat16
VMEM = pl.BlockSpec(memory_space=pltpu.VMEM)
HBM = pl.BlockSpec(memory_space=pltpu.HBM)
PARAMS = pltpu.CompilerParams(vmem_limit_bytes=16 * 2**20)
STEP = 32
SPAN = 2
MESSAGE = 18
EDGE = 16
TOGETHER = 4


def shift_down(block, count):
    return jnp.concatenate([jnp.zeros((count, block.shape[1]), block.dtype), block[:-count]], axis=0)


def inside(stream_ref, taps_ref, stream, padded):
    rows = stream_ref.shape[0]
    block = stream_ref[...].astype(F32)
    padded[8:, :] = block
    padded[6:8, :] = jnp.zeros((2, block.shape[1]), F32)
    out = taps_ref[stream, 0:1, :] * block
    out = out + taps_ref[stream, 1:2, :] * padded[7 : 7 + rows, :]
    return out + taps_ref[stream, 2:3, :] * padded[6 : 6 + rows, :]


def into_next(stream_ref, taps_ref, stream):
    last = stream_ref[stream_ref.shape[0] - 16 :, :].astype(F32)[14:]
    first = taps_ref[stream, 1:2, :] * last[1:] + taps_ref[stream, 2:3, :] * last[:1]
    return [first, taps_ref[stream, 2:3, :] * last[1:]]


def before_kernel(*refs):
    sources, (sent_ref, kept_gain_ref, padded, edges, *kept, sems) = refs[:7], refs[7:]
    loads = [pltpu.make_async_copy(a, b, sems.at[i]) for i, (a, b) in enumerate(zip(sources, kept, strict=True))]
    for load in loads:
        load.start()
    q_ref, k_ref, v_ref, taps_ref, filter_ref, bias_ref, gain_ref = kept
    for load in loads:
        load.wait()
    rows, channels = k_ref.shape
    groups = sent_ref.shape[0] // MESSAGE
    each = channels // groups
    key = inside(k_ref, taps_ref, 1, padded)
    value = inside(v_ref, taps_ref, 2, padded)
    signal = (key * value).T.reshape(groups, each, rows)
    down = lax.broadcasted_iota(jnp.int32, (rows, rows), 0)
    across = lax.broadcasted_iota(jnp.int32, (rows, rows), 1)
    backwards = (down + across == rows - 1).astype(BF16)
    taps = jnp.dot(backwards, filter_ref[...].astype(BF16), preferred_element_type=F32)
    taps = taps.T.reshape(groups, each, rows)
    start = q_ref[0:16, :].astype(F32)[0:2]
    first = taps_ref[0, 0:1, :] * start
    second = taps_ref[0, 1:2, :] * start[0:1]
    high = bias_ref[...].astype(BF16).astype(F32)
    middle = (bias_ref[...] - high).astype(BF16).astype(F32)
    low = bias_ref[...] - high - middle
    edge = [key[0:2], value[0:2], first[0:1], first[1:2] + second]
    for stream, ref in ((1, k_ref), (2, v_ref), (0, q_ref)):
        edge += into_next(ref, taps_ref, stream)
    edge += [high, middle, low, jnp.zeros((rows - 15, channels), F32)]
    edges[...] = jnp.concatenate(edge, axis=0).T
    edge = edges[pl.ds(0, groups, stride=each), :]
    for c in range(1, each):
        edge = edge + pltpu.roll(edges[pl.ds(c, groups, stride=each), :], EDGE * c, 1)
    rest = edge - edge.astype(BF16).astype(F32)
    messages = []
    for s in range(groups):
        messages += [signal[s], taps[s], edge[s : s + 1], rest[s : s + 1]]
    sent_ref[...] = jnp.concatenate(messages, axis=0).astype(BF16)
    kept_gain_ref[...] = gain_ref[...]


def conv_kernel(got_ref, out_ref, got, signal, edges, result, phased, *buffers):
    blocks, each, size = out_ref.shape
    step = STEP
    phases = size // step
    steps = blocks * phases
    several = len(buffers) // 2
    windows_refs, toeplitz_refs = buffers[:several], buffers[several:]
    got[...] = got_ref[...].astype(F32)
    lane = lax.broadcasted_iota(jnp.int32, (blocks, size), 1)
    own = lax.broadcasted_iota(jnp.int32, (step, size), 1) < lax.broadcasted_iota(jnp.int32, (step, size), 0) + (size + 1 - step)
    start = lane < 2
    parts = (lane[0:1, :] >= 8) & (lane[0:1, :] < 11)
    edge = got[pl.ds(2 * each, blocks, stride=MESSAGE), :] + got[pl.ds(2 * each + 1, blocks, stride=MESSAGE), :]
    edge = edge + jnp.where(lane % EDGE < 6, pltpu.roll(shift_down(edge, 1), size - 6, 1), 0.0)
    first = edge * pltpu.roll(edge, size - 2, 1)
    for c in range(each):
        at = slice(blocks * c, blocks * c + blocks)
        turned = pltpu.roll(first, size - EDGE * c, 1) if c else first
        signal[at, :] = jnp.where(start, turned, got[pl.ds(c, blocks, stride=MESSAGE), :])
        edges[at, :] = pltpu.roll(edge, (2 * size - EDGE * c - 4) % size, 1)
    for windows_ref in windows_refs:
        windows_ref[:16, :] = jnp.zeros((16, size), F32)

    phased[: phased.shape[0] - steps, :] = jnp.zeros((phased.shape[0] - steps, size), F32)

    def rows_of(c):
        return pl.ds(pl.multiple_of(blocks * c, blocks), blocks)

    def steps_of(c, windows_ref):
        now = signal[rows_of(c), :]
        for w in range(phases):
            left = size - step * w - step
            if left:
                turned = pltpu.roll(now, left, 1)
                windows_ref[pl.ds(16 + w, blocks, stride=phases), :] = jnp.where(lane < left, shift_down(turned, 1), turned)
            else:
                windows_ref[pl.ds(16 + w, blocks, stride=phases), :] = now

    def fill(c, toeplitz_ref):
        before = jnp.zeros((step, size), BF16)
        for d in range(blocks):
            spread = jnp.broadcast_to(got[pl.ds(MESSAGE * d + each + c, 1), :], (step, size))
            turned = pltpu.roll(spread, size + 1 - step, 1, stride=1, stride_axis=0).astype(BF16)
            g, back = divmod(d, SPAN)
            at = size * (SPAN - 1 - back)
            toeplitz_ref[step * g : step * g + step, at : at + size] = jnp.where(own, turned, before)
            before = turned

    def finish(c, windows_ref, toeplitz_ref):
        starts = [16 - phases * (SPAN - 1 - u) for u in range(SPAN)]
        windows = jnp.concatenate([windows_ref[a : a + steps, :] for a in starts], axis=1).astype(BF16)
        move = phases * SPAN
        group = size // step
        totals = jnp.zeros((steps, size), F32)
        wide = 2 * size
        for n in range(toeplitz_ref.shape[0] // wide):
            rows = steps - 2 * n * group * move
            product = lax.dot_general(
                windows[:rows],
                toeplitz_ref[wide * n : wide * n + wide, :],
                (((1,), (1,)), ((), ())),
                preferred_element_type=F32,
            )
            for half in range(2):
                count = (2 * n + half) * group * move
                part = product[: steps - count, size * half : size * half + size]
                totals = totals + (jnp.concatenate([jnp.zeros((count, size), F32), part], axis=0) if count else part)
        ahead = move * (group - 1)
        phased[ahead:, :] = totals
        out = None
        for r in range(phases):
            mine = None
            for i in range(group):
                source = phased[pl.ds(ahead - move * i + (i + r) % phases, blocks, stride=phases), :]
                mine = jnp.where(lane < step * i, mine, source) if i else source
            out = out + pltpu.roll(mine, step * r, 1) if r else mine
        edge = edges[rows_of(c), :]
        direct = jnp.sum(jnp.where(parts, edge[0:1, :], 0.0), axis=1, keepdims=True)
        mixed = out + direct * signal[rows_of(c), :]
        result[pl.ds(c, blocks, stride=each), :] = mixed * jnp.where(start, edge, 1.0)

    def channels(i, carry):
        for k in range(several):
            steps_of(several * i + k, windows_refs[k])
            fill(several * i + k, toeplitz_refs[k])
        for k in range(several):
            finish(several * i + k, windows_refs[k], toeplitz_refs[k])
        return carry

    lax.fori_loop(0, each // several, channels, 0)
    out_ref[...] = result[...].reshape(blocks, each, size).astype(BF16)


def mix_kernel(back_ref, q_ref, taps_ref, mixed_ref, squares_ref, padded):
    rows, channels = q_ref.shape
    query = inside(q_ref, taps_ref, 0, padded)
    back = back_ref[...].astype(F32).reshape(channels, rows).T
    row = lax.broadcasted_iota(jnp.int32, (rows, channels), 0)
    mixed = back * jnp.where(row < 2, 1.0, query)
    mixed_ref[...] = mixed
    sums = jnp.sum(mixed * mixed, axis=1, keepdims=True)
    squares_ref[...] = jnp.broadcast_to(sums, (rows, rows)).T[: squares_ref.shape[0]]


def norm_kernel(total, squares_ref, mixed_ref, gain_ref, rounded_ref, out_ref):
    rows = mixed_ref.shape[0]
    rounded_ref[...] = mixed_ref[...].astype(BF16)
    squares = jnp.sum(squares_ref[...], axis=0, keepdims=True)
    scale = lax.rsqrt(squares / total + EPS)
    scale = jnp.broadcast_to(scale, (rows, rows)).T[:, 0:1]
    out_ref[...] = (mixed_ref[...] * scale * gain_ref[...]).astype(BF16)


def shards(q_proj, k_proj, v_proj, feat_filter, long_filter, skip_bias, norm_gain):
    rows, channels = q_proj.shape
    groups = lax.axis_size("seq")
    columns = lax.axis_size("ch")
    each = channels // groups
    padded = pltpu.VMEM((rows + 8, channels), F32)
    sources = (q_proj, k_proj, v_proj, feat_filter, long_filter, skip_bias.reshape(1, channels), norm_gain.reshape(1, channels))
    sent, kept_gain = pl.pallas_call(
        before_kernel,
        out_shape=(
            jax.ShapeDtypeStruct((groups * MESSAGE, rows), BF16),
            jax.ShapeDtypeStruct((1, channels), F32),
        ),
        in_specs=[HBM] * 7,
        out_specs=(VMEM, VMEM),
        scratch_shapes=[padded, pltpu.VMEM((channels, rows), F32)] + [pltpu.VMEM(a.shape, a.dtype) for a in sources] + [pltpu.SemaphoreType.DMA((7,))],
        compiler_params=PARAMS,
        name="before",
    )(*(pltpu.with_memory_space_constraint(a, pltpu.HBM) for a in sources))
    sent = sent.reshape(groups, MESSAGE // 2, 2, rows)
    got = lax.all_to_all(sent, "seq", split_axis=0, concat_axis=0, tiled=True).reshape(groups * MESSAGE, rows)
    scratch = pltpu.VMEM((groups * each, rows), F32)
    conv = pl.pallas_call(
        conv_kernel,
        out_shape=jax.ShapeDtypeStruct((groups, each, rows), BF16),
        in_specs=[VMEM],
        out_specs=VMEM,
        scratch_shapes=[pltpu.VMEM((groups * MESSAGE, rows), F32)]
        + [scratch] * 3
        + [pltpu.VMEM((groups * rows // STEP + (rows // STEP - 1) * SPAN * rows // STEP, rows), F32)]
        + [pltpu.VMEM((groups * rows // STEP + 16, rows), F32)] * TOGETHER
        + [pltpu.VMEM((STEP * groups // SPAN, SPAN * rows), BF16)] * TOGETHER,
        compiler_params=PARAMS,
        name="conv",
    )(got)
    back = lax.all_to_all(conv, "seq", split_axis=0, concat_axis=0, tiled=True)
    mixed, squares = pl.pallas_call(
        mix_kernel,
        out_shape=(
            jax.ShapeDtypeStruct((rows, channels), F32),
            jax.ShapeDtypeStruct((columns, rows), F32),
        ),
        in_specs=[VMEM] * 3,
        out_specs=(VMEM, VMEM),
        scratch_shapes=[padded],
        compiler_params=PARAMS,
        name="mix",
    )(back, q_proj, feat_filter)
    squares = lax.all_to_all(squares, "ch", split_axis=0, concat_axis=0, tiled=True)
    rounded, normed = pl.pallas_call(
        lambda *refs: norm_kernel(float(columns * channels), *refs),
        out_shape=(jax.ShapeDtypeStruct((rows, channels), BF16),) * 2,
        in_specs=[VMEM] * 3,
        out_specs=(VMEM, VMEM),
        compiler_params=PARAMS,
        name="norm",
    )(squares, mixed, kept_gain)
    return (rounded, normed)


def solution(mesh):
    return jax.shard_map(
        shards,
        mesh=mesh,
        in_specs=(
            P("seq", "ch"),
            P("seq", "ch"),
            P("seq", "ch"),
            P(None, None, "ch"),
            P("seq", "ch"),
            P("ch"),
            P("ch"),
        ),
        out_specs=(P("seq", "ch"), P("seq", "ch")),
        check_vma=False,
    )
```
